32 devices in a mesh: dp: 8 (over z, x), tensor: 4 (over y, core).
Axes of the slice: x: 2, y: 2, z: 4, core: 2. Of those that a mesh axis runs over, the one named last changes fastest.
Arguments:
- context: bfloat16 [2, 8192, 3072], P(None, 'dp', 'tensor'), may hold values from -6 to 6
- out_grad: bfloat16 [2, 8192, 3072], P(None, ('dp', 'tensor')), may hold values from -0.1875 to 0.1875
- error_in: bfloat16 [2, 24576, 3072], P(None, 'dp', 'tensor'), may hold values from -6 to 6
- right_init: float32 [2, 64, 3072], P(None, None, 'tensor'), may hold values from -6 to 6
Outputs:
- summed_update: bfloat16 [2, 3072, 3072], P(None, 'dp', 'tensor')
- error_out: bfloat16 [2, 24576, 3072], P(None, 'dp', 'tensor')
The draws below stay inside these ranges and needn't reach their ends.
All inputs are finite; a program needn't handle non-finite values.
Results may differ from the reference program's by a relative error of at most 0.015.
Values may be sent and summed in bfloat16 or wider, within the bound.
A program may use at most 128 MiB of HBM per device.

```python
import jax
import jax.numpy as jnp
from jax import lax

D = 3072
RANK = 64
LAYERS = 2
TOK_DEV = 1024
TOKENS = 8192
REPL_ROWS = 24576
N_DP = 8


def block_levels(key, shape, pieces, least, high):
    loudness = 1.0
    for dim, blocks in pieces:
        heights = jax.random.uniform(jax.random.fold_in(jax.random.fold_in(key, 6), dim), (blocks,), jnp.float32, least / len(pieces), high / len(pieces))
        loudness = loudness * jnp.repeat(jnp.exp(heights), shape[dim] // blocks).reshape((-1,) + (1,) * (len(shape) - 1 - dim))
    return loudness


def scatter_about(rng, dims, deviation, bound, split=(), held_as=jnp.bfloat16):
    result = jax.random.normal(rng, dims, jnp.float32) * deviation
    if len(split) > 0:
        result = block_levels(rng, dims, split, -0.22, 0.18) * result
    return jnp.clip(result, min=-bound, max=bound).astype(held_as)


def setup_inputs(seed: int = 0) -> dict:
    keys = jax.random.split(jax.random.key(seed), 5)
    context = scatter_about(keys[0], (LAYERS, TOKENS, D), 1.0, 6.0, ((1, 8), (2, 4)))
    out_grad = scatter_about(keys[1], (LAYERS, TOKENS, D), TOK_DEV ** -0.5, 0.1875, ((1, 32),))
    error_in = scatter_about(keys[2], (LAYERS, REPL_ROWS, D), 1.0, 6.0, ((1, 8), (2, 4)))
    right_init = scatter_about(keys[3], (LAYERS, RANK, D), 1.0, 6.0, ((2, 4),), jnp.float32)
    return {"context": context, "out_grad": out_grad, "error_in": error_in, "right_init": right_init}


def ortho_rows(left_factor):
    gram_matrix = jnp.dot(left_factor, left_factor.T, precision=lax.Precision.HIGHEST)
    ridge_term = 1e-06 * jnp.mean(jnp.diagonal(gram_matrix))
    gram_matrix = gram_matrix + ridge_term * jnp.eye(gram_matrix.shape[0], dtype=gram_matrix.dtype)
    factor_low = jnp.linalg.cholesky(gram_matrix)
    return jax.scipy.linalg.solve_triangular(factor_low, left_factor, lower=True)

def reference(context, out_grad, error_in, right_init):
    summed_list = []
    error_list = []
    for layer in range(LAYERS):
        ctx_blocks = context[layer].reshape(N_DP, TOK_DEV, D)
        grad_blocks = out_grad[layer].reshape(N_DP, TOK_DEV, D)
        err_blocks = error_in[layer].reshape(N_DP, D, D)

        def one_moment(items):
            return jnp.dot(items[1].T.astype(jnp.float32), items[0].astype(jnp.float32), preferred_element_type=jnp.float32) + items[2].astype(jnp.float32)
        moments = lax.map(one_moment, (ctx_blocks, grad_blocks, err_blocks))
        left_factor = jnp.einsum('re,nde->rd', right_init[layer], moments, precision=lax.Precision.HIGHEST)
        ortho_basis = ortho_rows(left_factor)
        right_factor = jnp.einsum('rd,nde->re', ortho_basis, moments, precision=lax.Precision.HIGHEST)
        summed = jnp.dot(ortho_basis.T, right_factor, precision=lax.Precision.HIGHEST)
        summed_list.append(summed.astype(jnp.bfloat16))
        mean_part = jnp.dot(ortho_basis.T, right_factor / N_DP, precision=lax.Precision.HIGHEST)
        new_error = (moments - mean_part[None]).astype(jnp.bfloat16)
        error_list.append(new_error.reshape(N_DP * D, D))
    return (jnp.stack(summed_list), jnp.stack(error_list))
```

```python
import functools

import jax
import jax.numpy as jnp
from jax import lax
from jax.experimental import pallas as pl
from jax.experimental.pallas import tpu as pltpu
from jax.sharding import PartitionSpec as P

MESH = pl.DeviceIdType.MESH
HIGHEST = lax.Precision.HIGHEST
F32 = jnp.float32
BF16 = jnp.bfloat16
WIRE = jnp.bfloat16
ROWS = 16
TAIL = 32
BLOCKS = 6
PLAN = (3, 6, 2, 5)


def split(value):
    high = value.astype(BF16)
    return high, (value - high.astype(F32)).astype(BF16)


def dot(a, b, dims):
    return lax.dot_general(a, b, (dims, ((), ())), preferred_element_type=F32)


def inverse_factors(grams):
    size = grams[0].shape[0]
    rows = lax.broadcasted_iota(jnp.int32, (size, size), 0)
    cols = lax.broadcasted_iota(jnp.int32, (size, size), 1)
    eye = (rows == cols).astype(F32)
    wide_rows = lax.broadcasted_iota(jnp.int32, (size, 2 * size), 0)
    work = []
    for gram in grams:
        mean = jnp.sum(jnp.sum(gram * eye, axis=1, keepdims=True), axis=0, keepdims=True) / size
        work.append(jnp.concatenate([gram + (1e-06 * mean) * eye, eye], axis=1))
    scales = [jnp.zeros((size, 1), F32) for _ in grams]
    one_col = wide_rows[:, :1]
    for k in range(size):
        for i, full in enumerate(work):
            row = full[k : k + 1, :]
            pivot = full[k : k + 1, k : k + 1]
            ratio = jnp.where(one_col > k, full[:, k : k + 1] / pivot, 0.0)
            scales[i] = jnp.where(one_col == k, lax.rsqrt(pivot), scales[i])
            work[i] = full - ratio * row
    return [full[:, size:] * scale for full, scale in zip(work, scales)]


def fold(parts, rank):
    if len(parts) == 2:
        first = lax.broadcasted_iota(jnp.int32, (1, 2 * rank), 1) < rank
        kept = jnp.where(first, parts[0], parts[1])
        moved = jnp.where(first, parts[1], parts[0])
        return kept + pltpu.roll(moved, rank, 1)
    return jnp.concatenate([part[:, :rank] + part[:, rank:] for part in parts], axis=1)


def comm_kernel(
    n_d,
    n_t,
    x_hbm,
    y_hbm,
    e_hbm,
    r_hbm,
    m_ref,
    sum_ref,
    yt_ref,
    xt_ref,
    x_ref,
    y_chip,
    y_far,
    r_ref,
    pt,
    pt_core,
    pt_send,
    pt_in,
    q_own,
    q_far,
    lt,
    lt_core,
    lt_send,
    lt_in,
    lt_y,
    lt_sum,
    ltf,
    r_send,
    r_in,
    r_all,
    s_all,
    t_err,
    local_sems,
    e_sems,
    y_send,
    y_recv,
    f_send,
    f_recv,
    own_sems,
    p_send,
    p_recv,
    pc_sems,
    c_sems,
    d_send,
    d_recv,
    s_send,
    s_recv,
    g_send,
    g_recv,
    h_send,
    h_recv,
    q_send,
    q_recv,
    qf_send,
    qf_recv,
    a_send,
    a_recv,
    b_send,
    b_recv,
):
    layers, own, width = y_hbm.shape
    tokens, feats = x_ref.shape[1:]
    rank = r_ref.shape[1]
    wide = layers * rank
    d = lax.axis_index("dp")
    t = lax.axis_index("tensor")
    core = lax.rem(t, 2)
    place = lax.div(t, 2)
    partner = t + 1 - 2 * core
    n_y = n_t // 2
    half = width // 2
    piece = half // n_d
    block_rows = width // BLOCKS
    pair = 2 * own
    per_layer = own // ROWS
    tail = TAIL
    main = own - tail

    def remote(src, dst, send, recv, where):
        return pltpu.make_async_remote_copy(
            src_ref=src, dst_ref=dst, send_sem=send, recv_sem=recv, device_id=where, device_id_type=MESH
        )

    my_rows = pl.ds(pl.multiple_of(core * own, own), own)
    partner_rows = pl.ds(pl.multiple_of((1 - core) * own, own), own)

    barrier = pltpu.get_barrier_semaphore()
    for k in range(1, n_d):
        pl.semaphore_signal(barrier, inc=1, device_id={"dp": lax.rem(d + k, n_d)}, device_id_type=MESH)
    for k in range(1, n_t):
        pl.semaphore_signal(barrier, inc=1, device_id={"tensor": lax.rem(t + k, n_t)}, device_id_type=MESH)
    r_load = pltpu.make_async_copy(r_hbm, r_ref, local_sems.at[0])
    x_load = pltpu.make_async_copy(x_hbm, x_ref, local_sems.at[1])
    y_load = pltpu.make_async_copy(y_hbm, y_chip.at[:, my_rows, :], local_sems.at[2])
    r_load.start()
    x_load.start()
    e_loads = []
    for side in range(2):
        at = pl.ds(side * half, half)
        for layer in range(layers):
            e_loads.append(
                pltpu.make_async_copy(e_hbm.at[layer, at, :], m_ref.at[layer, at, :], e_sems.at[side, layer])
            )
    for load in e_loads[:layers]:
        load.start()
    y_load.start()
    for load in e_loads[layers:]:
        load.start()
    with jax.named_scope("bar"):
        pl.semaphore_wait(barrier, n_d + n_t - 2)
    chunks = [(layer, c) for layer in range(layers) for c in range(per_layer)]
    total_chunks = len(chunks)

    def landing(i, m, side):
        layer, c = chunks[i]
        if layer == layers - 1 and c * ROWS >= main:
            return yt_ref.at[m - 1, side, pl.ds(c * ROWS - main, ROWS), :]
        return y_far.at[layer, m - 1, side, pl.ds(c * ROWS, ROWS), :]

    def chunk_copy(i, m):
        layer, c = chunks[i]
        return remote(
            y_hbm.at[layer, pl.ds(c * ROWS, ROWS), :],
            landing(i, m, core),
            y_send.at[m - 1, i],
            y_recv.at[m - 1, i],
            {"tensor": lax.rem(t + 2 * m, n_t)},
        )

    def forward_copy(i, m):
        here = landing(i, m, core)
        return remote(here, here, f_send.at[m - 1, i], f_recv.at[m - 1, i], {"tensor": partner})

    def forward_in(i, m):
        here = landing(i, m, 1 - core)
        return remote(here, here, f_send.at[m - 1, i], f_recv.at[m - 1, i], {"tensor": partner})

    sent = [0]
    passed = [0]
    needed = [0]

    def send_chunks(count):
        stop = min(sent[0] + count, total_chunks)
        for i in range(sent[0], stop):
            for m in range(1, n_y):
                chunk_copy(i, m).start()
        sent[0] = stop

    def pass_chunks(upto):
        for i in range(passed[0], min(upto, sent[0])):
            for m in range(1, n_y):
                chunk_copy(i, m).wait_recv()
                forward_copy(i, m).start()
        passed[0] = max(passed[0], min(upto, sent[0]))

    def need_chunks(upto):
        pass_chunks(upto)
        for i in range(needed[0], upto):
            for m in range(1, n_y):
                forward_in(i, m).wait_recv()
        needed[0] = max(needed[0], upto)

    send_chunks(PLAN[0])
    own_copy = remote(y_hbm, y_chip.at[:, my_rows, :], own_sems.at[0], own_sems.at[1], {"tensor": partner})
    own_copy.start()
    own_in = remote(y_hbm, y_chip.at[:, partner_rows, :], own_sems.at[0], own_sems.at[1], {"tensor": partner})

    def far_place(m):
        return lax.rem(place + n_y - m, n_y)

    r_load.wait()
    x_load.wait()
    r_parts = []
    for layer in range(layers):
        high, low = split(r_ref[layer])
        r_parts.append(jnp.concatenate([high, low] if layer % 2 == 0 else [low, high], axis=0))
    with jax.named_scope("token_terms"):
        for side in range(2):
            for other in range(n_y):
                at = pl.ds((2 * other + side) * own, own)
                parts = [dot(x_ref[layer, at, :], r_parts[layer], ((1,), (1,))) for layer in range(layers)]
                pt[side, other] = fold(parts, rank)
    pc_copy = remote(pt.at[1 - core], pt_core, pc_sems.at[0], pc_sems.at[1], {"tensor": partner})
    pc_copy.start()
    pc_copy.wait()
    p_total = None
    for m in range(1, n_y):
        there = lax.rem(place + m, n_y)
        pt_send[m - 1] = (pt[core, there] + pt_core[there]).astype(WIRE)
    p_out = []
    for m in range(1, n_y):
        copy = remote(
            pt_send.at[m - 1], pt_in.at[m - 1], p_send.at[m - 1], p_recv.at[m - 1], {"tensor": lax.rem(t + 2 * m, n_t)}
        )
        copy.start()
        p_out.append(copy)
    send_chunks(PLAN[1])
    p_total = pt[core, place] + pt_core[place]

    with jax.named_scope("left_of_error"):
        for side in range(2):
            for load in e_loads[side * layers : (side + 1) * layers]:
                load.wait()

            def left_of_error(i, carry):
                at = pl.ds(pl.multiple_of(side * half + i * block_rows, block_rows), block_rows)
                parts = [dot(m_ref[layer, at, :], r_parts[layer], ((1,), (1,))) for layer in range(layers)]
                lt[at, :] = fold(parts, rank)
                return carry

            lax.fori_loop(0, BLOCKS // 2, left_of_error, 0)
    y_load.wait()
    with jax.named_scope("token_wait"):
        for copy in p_out:
            copy.wait()
    for m in range(1, n_y):
        p_total = p_total + pt_in[m - 1].astype(F32)
    p_high = p_total.astype(BF16).astype(F32)
    p_low = p_total - p_high
    if layers == 2:
        first = lax.broadcasted_iota(jnp.int32, (1, wide), 1) < rank
        turned = pltpu.roll(p_low, rank, 1)
        p_parts = [jnp.where(first, p_high, turned).astype(BF16), jnp.where(first, turned, p_high).astype(BF16)]
    else:
        p_parts = [
            jnp.concatenate([part[:, k * rank : (k + 1) * rank] for part in (p_high, p_low)], axis=1).astype(BF16)
            for k in range(layers)
        ]

    mine = pl.multiple_of(core * half, half)
    other = pl.multiple_of((1 - core) * half, half)

    def left_of_tokens(start):
        def step(i, carry):
            at = pl.ds(pl.multiple_of(start + i * block_rows, block_rows), block_rows)
            parts = [dot(y_chip[layer, my_rows, at], p_parts[layer], ((0,), (0,))) for layer in range(layers)]
            lt[at, :] += fold(parts, rank)
            return carry

        lax.fori_loop(0, BLOCKS // 2, step, 0)

    core_copy = remote(lt.at[pl.ds(other, half), :], lt_core, c_sems.at[0], c_sems.at[1], {"tensor": partner})
    with jax.named_scope("left_of_tokens"):
        left_of_tokens(other)
        core_copy.start()
        left_of_tokens(mine)
    with jax.named_scope("core_wait"):
        core_copy.wait()

    def add_core(j, carry):
        at = pl.ds(pl.multiple_of(mine + j * piece, piece), piece)
        value = lt[at, :] + lt_core[pl.ds(pl.multiple_of(j * piece, piece), piece), :]
        lt_send[j] = value.astype(lt_send.dtype)
        return carry

    lax.fori_loop(0, n_d, add_core, 0)
    d_out = []
    for k in range(1, n_d):
        there = lax.rem(d + k, n_d)
        copy = remote(lt_send.at[there], lt_in.at[k - 1], d_send.at[k - 1], d_recv.at[k - 1], {"dp": there})
        copy.start()
        d_out.append(copy)
    send_chunks(PLAN[2])

    def moment_of_chip(layer):
        tokens_here = pl.ds(pl.multiple_of(place * pair, pair), pair)

        def step(i, carry):
            at = pl.ds(pl.multiple_of(i * block_rows, block_rows), block_rows)
            term = dot(y_chip[layer, :, at], x_ref[layer, tokens_here, :], ((0,), (0,)))
            m_ref[layer, at, :] = (m_ref[layer, at, :].astype(F32) + term).astype(BF16)
            return carry

        with jax.named_scope("moment"):
            lax.fori_loop(0, BLOCKS, step, 0)

    own_in.wait_recv()
    moment_of_chip(0)
    with jax.named_scope("dp_wait"):
        for copy in d_out:
            copy.wait()
    total = lt_send[d].astype(F32)
    for k in range(n_d - 1):
        total = total + lt_in[k].astype(F32)
    lt_sum[...] = total
    s_out = []
    for m in range(1, n_y):
        copy = remote(lt_sum, lt_y.at[m - 1], s_send.at[m - 1], s_recv.at[m - 1], {"tensor": lax.rem(t + 2 * m, n_t)})
        copy.start()
        s_out.append(copy)
    send_chunks(PLAN[3])
    with jax.named_scope("sum_wait"):
        for copy in s_out:
            copy.wait()
    total = lt_sum[...]
    for m in range(n_y - 1):
        total = total + lt_y[m]

    def slot(side, index):
        return ltf.at[pl.ds(pl.multiple_of(side * half + index * piece, piece), piece), :]

    ltf[pl.ds(pl.multiple_of(mine + d * piece, piece), piece), :] = total.astype(ltf.dtype)
    g_out = []
    for k in range(1, n_d):
        there = lax.rem(d + k, n_d)
        copy = remote(slot(core, d), slot(core, d), g_send.at[k - 1], g_recv.at[k - 1], {"dp": there})
        copy.start()
        g_out.append(copy)
    for layer in range(1, layers):
        moment_of_chip(layer)
    h_out = []
    with jax.named_scope("gather_wait"):
        for k in range(n_d):
            source = lax.rem(d + n_d - k, n_d)
            if k > 0:
                remote(
                    slot(core, source), slot(core, source), g_send.at[k - 1], g_recv.at[k - 1], {"dp": source}
                ).wait_recv()
            copy = remote(slot(core, source), slot(core, source), h_send.at[k], h_recv.at[k], {"tensor": partner})
            copy.start()
            h_out.append(copy)
        for k in range(n_d):
            source = lax.rem(d + n_d - k, n_d)
            remote(
                slot(1 - core, source), slot(1 - core, source), h_send.at[k], h_recv.at[k], {"tensor": partner}
            ).wait_recv()

    lanes = lax.broadcasted_iota(jnp.int32, (1, wide), 1) // rank
    sublanes = lax.broadcasted_iota(jnp.int32, (wide, 1), 0) // rank

    def merge(parts, index):
        value = parts[0]
        for layer in range(1, layers):
            value = jnp.where(index == layer, parts[layer], value)
        return value

    with jax.named_scope("token_right"):
        q_own[...] = merge(
            [dot(y_chip[layer, my_rows, :], ltf[...], ((1,), (0,))) for layer in range(layers)], lanes
        ).astype(q_own.dtype)
    q_out = []
    for m in range(1, n_y):
        copy = remote(
            q_own, q_far.at[m - 1, core], q_send.at[m - 1], q_recv.at[m - 1], {"tensor": lax.rem(t + 2 * m, n_t)}
        )
        copy.start()
        q_out.append(copy)
    send_chunks(total_chunks)
    with jax.named_scope("right_of_chip"):
        right = merge([dot(ltf[...], m_ref[layer], ((0,), (0,))) for layer in range(layers)], sublanes)
    with jax.named_scope("token_right_wait"):
        q_pass = []
        for m in range(1, n_y):
            here = q_far.at[m - 1, core]
            remote(q_own, here, q_send.at[m - 1], q_recv.at[m - 1], {"tensor": lax.rem(t + 2 * m, n_t)}).wait_recv()
            copy = remote(here, here, qf_send.at[m - 1], qf_recv.at[m - 1], {"tensor": partner})
            copy.start()
            q_pass.append(copy)
        for m in range(1, n_y):
            here = q_far.at[m - 1, 1 - core]
            remote(here, here, qf_send.at[m - 1], qf_recv.at[m - 1], {"tensor": partner}).wait_recv()
    for m in range(1, n_y):
        at = pl.ds(pl.multiple_of(far_place(m) * pair, pair), pair)
        basis = q_far[m - 1].reshape(pair, wide)
        right = right + merge(
            [dot(basis, x_ref[layer, at, :], ((0,), (0,))) for layer in range(layers)], sublanes
        )
    share = wide // n_d
    for j in range(n_d):
        r_send[j] = right[j * share : (j + 1) * share, :].astype(BF16)
    a_out = []
    for k in range(1, n_d):
        there = lax.rem(d + k, n_d)
        copy = remote(r_send.at[there], r_in.at[k - 1], a_send.at[k - 1], a_recv.at[k - 1], {"dp": there})
        copy.start()
        a_out.append(copy)

    with jax.named_scope("inverse"):
        gram = dot(ltf[...], ltf[...], ((0,), (0,)))
        grams = [gram[k * rank : (k + 1) * rank, k * rank : (k + 1) * rank] for k in range(layers)]
        inverses = [
            lax.dot_general(
                factor, factor, (((0,), (0,)), ((), ())), precision=HIGHEST, preferred_element_type=F32
            )
            for factor in inverse_factors(grams)
        ]
    with jax.named_scope("right_wait"):
        for copy in a_out:
            copy.wait()
    total = r_send[d].astype(F32)
    for k in range(n_d - 1):
        total = total + r_in[k].astype(F32)
    r_all[d] = total.astype(BF16)
    b_out = []
    for k in range(1, n_d):
        copy = remote(r_all.at[d], r_all.at[d], b_send.at[k - 1], b_recv.at[k - 1], {"dp": lax.rem(d + k, n_d)})
        copy.start()
        b_out.append(copy)
    pass_chunks(per_layer)
    with jax.named_scope("right_gather_wait"):
        for k in range(1, n_d):
            source = lax.rem(d + n_d - k, n_d)
            remote(r_all.at[source], r_all.at[source], b_send.at[k - 1], b_recv.at[k - 1], {"dp": source}).wait_recv()
    for j in range(n_d):
        s_all[j * share : (j + 1) * share, :] = r_all[j].astype(F32)
    t_err[...] = jnp.zeros_like(t_err)
    for layer in range(layers):
        rows = pl.ds(layer * rank, rank)
        scaled = lax.dot_general(
            inverses[layer],
            s_all[layer * rank : (layer + 1) * rank, :],
            (((1,), (0,)), ((), ())),
            precision=HIGHEST,
            preferred_element_type=F32,
        )
        high, low = split(scaled * (-1.0 / n_d))
        t_err[layer, layer * rank : (layer + 1) * rank, :] = high
        t_err[layer, wide + layer * rank : wide + (layer + 1) * rank, :] = low

    def low_rank(at, layer):
        basis = ltf[at, :]
        return dot(jnp.concatenate([basis, basis], axis=1), t_err[layer], ((1,), (0,)))

    def add_far(layer, start, stop, with_rank):
        def step(i, carry):
            at = pl.ds(pl.multiple_of(i * block_rows, block_rows), block_rows)
            value = m_ref[layer, at, :].astype(F32)
            if with_rank:
                value = value + low_rank(at, layer)
            for m in range(1, n_y):
                base = far_place(m) * pair
                if stop - start == own:
                    rows = pl.ds(pl.multiple_of(base, pair), pair)
                    y_rows = y_far[layer, m - 1, :, :, at].reshape(pair, block_rows)
                    value = value + dot(y_rows, x_ref[layer, rows, :], ((0,), (0,)))
                else:
                    for side in range(2):
                        rows = pl.ds(pl.multiple_of(base + side * own + start, 16), stop - start)
                        y_rows = y_far[layer, m - 1, side, start:stop, at]
                        value = value + dot(y_rows, x_ref[layer, rows, :], ((0,), (0,)))
            m_ref[layer, at, :] = value.astype(BF16)
            return carry

        with jax.named_scope("far_terms"):
            lax.fori_loop(0, BLOCKS, step, 0)

    for layer in range(layers - 1):
        need_chunks((layer + 1) * per_layer)
        add_far(layer, 0, own, True)
    own_rows = width // n_d
    for layer in range(layers):
        value = low_rank(pl.ds(pl.multiple_of(d * own_rows, own_rows), own_rows), layer)
        sum_ref[layer] = (value * (-1.0 * n_d)).astype(sum_ref.dtype)
    for m in range(1, n_y):
        for side in range(2):
            rows = pl.ds(pl.multiple_of(far_place(m) * pair + side * own + main, 16), tail)
            xt_ref[m - 1, side] = x_ref[layers - 1, rows, :]
    last = (layers - 1) * per_layer
    with jax.named_scope("far_wait"):
        for i in range(last, last + main // ROWS):
            pass_chunks(i + 1)
        need_chunks(last + main // ROWS)
    add_far(layers - 1, 0, main, True)
    with jax.named_scope("tail_wait"):
        for i in range(last + main // ROWS, total_chunks):
            pass_chunks(i + 1)
        need_chunks(total_chunks)
    own_copy.wait_send()
    for copy in g_out + h_out + q_out + q_pass + b_out:
        copy.wait_send()
    for i in range(total_chunks):
        for m in range(1, n_y):
            chunk_copy(i, m).wait_send()
            forward_copy(i, m).wait_send()


def finish_kernel(m_ref, sum_ref, yt_ref, xt_ref, err_hbm, out_hbm, stage, m_sems, sum_sem, block_sems):
    layers, width, feats = m_ref.shape
    block_rows = width // BLOCKS
    copies = [pltpu.make_async_copy(m_ref.at[layer], err_hbm.at[layer], m_sems.at[layer]) for layer in range(layers - 1)]
    copies.append(pltpu.make_async_copy(sum_ref, out_hbm, sum_sem))
    for copy in copies:
        copy.start()
    rows = xt_ref.shape[0] * xt_ref.shape[1] * xt_ref.shape[2]
    x_rows = xt_ref[...].reshape(rows, feats)
    for i in range(BLOCKS):
        at = pl.ds(i * block_rows, block_rows)
        term = dot(yt_ref[:, :, :, at].reshape(rows, block_rows), x_rows, ((0,), (0,)))
        stage[at, :] = (m_ref[layers - 1, at, :].astype(F32) + term).astype(stage.dtype)
        copy = pltpu.make_async_copy(stage.at[at, :], err_hbm.at[layers - 1, at, :], block_sems.at[i])
        copy.start()
        copies.append(copy)
    for copy in copies:
        copy.wait()


def solution(mesh):
    n_d, n_t = mesh.shape["dp"], mesh.shape["tensor"]

    def body(context, out_grad, error_in, right_init):
        layers, tokens, feats = context.shape
        own, width = out_grad.shape[1:]
        rank = right_init.shape[1]
        wide = layers * rank
        half = width // 2
        piece = half // n_d
        share = wide // n_d
        n_y = n_t // 2
        far = max(n_y - 1, 1)
        n_c = layers * (own // ROWS)
        rows = width // n_d
        dma = pltpu.SemaphoreType.DMA
        any_spec = pl.BlockSpec(memory_space=pl.ANY)
        vmem_spec = pl.BlockSpec(memory_space=pltpu.VMEM)
        pairs = lambda *shape: [dma(shape), dma(shape)]
        moment, summed, y_tail, x_tail = pl.pallas_call(
            functools.partial(comm_kernel, n_d, n_t),
            name="low_rank_chain",
            out_shape=(
                pltpu.VMEM((layers, width, feats), BF16),
                pltpu.VMEM((layers, rows, feats), BF16),
                pltpu.VMEM((far, 2, TAIL, width), BF16),
                pltpu.VMEM((far, 2, TAIL, feats), BF16),
            ),
            in_specs=[any_spec] * 4,
            out_specs=(vmem_spec,) * 4,
            scratch_shapes=[
                pltpu.VMEM((layers, tokens, feats), BF16),
                pltpu.VMEM((layers, 2 * own, width), BF16),
                pltpu.VMEM((layers, far, 2, own, width), BF16),
                pltpu.VMEM((layers, rank, feats), F32),
                pltpu.VMEM((2, n_y, own, wide), F32),
                pltpu.VMEM((n_y, own, wide), F32),
                pltpu.VMEM((far, own, wide), WIRE),
                pltpu.VMEM((far, own, wide), WIRE),
                pltpu.VMEM((own, wide), WIRE),
                pltpu.VMEM((far, 2, own, wide), WIRE),
                pltpu.VMEM((width, wide), F32),
                pltpu.VMEM((half, wide), F32),
                pltpu.VMEM((n_d, piece, wide), WIRE),
                pltpu.VMEM((n_d - 1, piece, wide), WIRE),
                pltpu.VMEM((far, piece, wide), F32),
                pltpu.VMEM((piece, wide), F32),
                pltpu.VMEM((width, wide), WIRE),
                pltpu.VMEM((n_d, share, feats), BF16),
                pltpu.VMEM((n_d - 1, share, feats), BF16),
                pltpu.VMEM((n_d, share, feats), BF16),
                pltpu.VMEM((wide, feats), F32),
                pltpu.VMEM((layers, 2 * wide, feats), BF16),
                dma((3,)),
                dma((2, layers)),
            ]
            + pairs(far, n_c)
            + pairs(far, n_c)
            + [dma((2,))]
            + pairs(far)
            + [dma((2,)), dma((2,))]
            + pairs(n_d - 1)
            + pairs(far)
            + pairs(n_d - 1)
            + pairs(n_d)
            + pairs(far)
            + pairs(far)
            + pairs(n_d - 1)
            + pairs(n_d - 1),
            compiler_params=pltpu.CompilerParams(
                collective_id=0, has_side_effects=True, vmem_limit_bytes=40 * 1024 * 1024
            ),
        )(*(pltpu.with_memory_space_constraint(a, pltpu.HBM) for a in (context, out_grad, error_in, right_init)))
        new_error, total = pl.pallas_call(
            finish_kernel,
            name="new_error",
            in_specs=[vmem_spec] * 4,
            out_specs=(any_spec, any_spec),
            out_shape=(
                jax.ShapeDtypeStruct((layers, width, feats), BF16),
                jax.ShapeDtypeStruct((layers, rows, feats), BF16),
            ),
            scratch_shapes=[pltpu.VMEM((width, feats), BF16), dma((layers,)), dma, dma((BLOCKS,))],
            compiler_params=pltpu.CompilerParams(vmem_limit_bytes=16 * 1024 * 1024),
        )(moment, summed, y_tail, x_tail)
        return total, new_error

    return jax.shard_map(
        body,
        mesh=mesh,
        in_specs=(
            P(None, "dp", "tensor"),
            P(None, ("dp", "tensor"), None),
            P(None, "dp", "tensor"),
            P(None, None, "tensor"),
        ),
        out_specs=(P(None, "dp", "tensor"), P(None, "dp", "tensor")),
        check_vma=False,
    )
```

```python
import functools

import jax
import jax.numpy as jnp
from jax import lax
from jax.experimental import pallas as pl
from jax.experimental.pallas import tpu as pltpu
from jax.sharding import PartitionSpec as P

MESH = pl.DeviceIdType.MESH
HIGHEST = lax.Precision.HIGHEST
F32 = jnp.float32
BF16 = jnp.bfloat16
WIRE = jnp.bfloat16
ROWS = 16
LAST_ROWS = 16
TAIL = 32
PASSED = 9
BLOCKS = 6
PLAN = (3, 6, 4, 7)


def split(value):
    high = value.astype(BF16)
    return high, (value - high.astype(F32)).astype(BF16)


def dot(a, b, dims):
    return lax.dot_general(a, b, (dims, ((), ())), preferred_element_type=F32)


def inverse_factors(grams):
    size = grams[0].shape[0]
    rows = lax.broadcasted_iota(jnp.int32, (size, size), 0)
    cols = lax.broadcasted_iota(jnp.int32, (size, size), 1)
    eye = (rows == cols).astype(F32)
    wide_rows = lax.broadcasted_iota(jnp.int32, (size, 2 * size), 0)
    work = []
    for gram in grams:
        mean = jnp.sum(jnp.sum(gram * eye, axis=1, keepdims=True), axis=0, keepdims=True) / size
        work.append(jnp.concatenate([gram + (1e-06 * mean) * eye, eye], axis=1))
    scales = [jnp.zeros((size, 1), F32) for _ in grams]
    one_col = wide_rows[:, :1]
    for k in range(size):
        for i, full in enumerate(work):
            row = full[k : k + 1, :]
            pivot = full[k : k + 1, k : k + 1]
            ratio = jnp.where(one_col > k, full[:, k : k + 1] / pivot, 0.0)
            scales[i] = jnp.where(one_col == k, lax.rsqrt(pivot), scales[i])
            work[i] = full - ratio * row
    return [full[:, size:] * scale for full, scale in zip(work, scales)]


def fold(parts, rank):
    if len(parts) == 2:
        first = lax.broadcasted_iota(jnp.int32, (1, 2 * rank), 1) < rank
        kept = jnp.where(first, parts[0], parts[1])
        moved = jnp.where(first, parts[1], parts[0])
        return kept + pltpu.roll(moved, rank, 1)
    return jnp.concatenate([part[:, :rank] + part[:, rank:] for part in parts], axis=1)


def comm_kernel(
    n_d,
    n_t,
    x_hbm,
    y_hbm,
    e_hbm,
    r_hbm,
    m_ref,
    sum_ref,
    yt_ref,
    xt_ref,
    x_ref,
    y_chip,
    y_far,
    r_ref,
    pt,
    pt_core,
    pt_send,
    pt_in,
    q_own,
    q_far,
    lt,
    lt_core,
    lt_send,
    lt_in,
    lt_y,
    lt_sum,
    ltf,
    r_send,
    r_in,
    r_all,
    s_all,
    t_err,
    local_sems,
    e_sems,
    y_send,
    y_recv,
    f_send,
    f_recv,
    own_sems,
    p_send,
    p_recv,
    pc_sems,
    c_sems,
    d_sems,
    s_send,
    s_recv,
    g_send,
    g_recv,
    h_sems,
    q_send,
    q_recv,
    qf_send,
    qf_recv,
    a_sems,
    b_sems,
    go_tensor,
    go_dp,
):
    layers, own, width = y_hbm.shape
    tokens, feats = x_ref.shape[1:]
    rank = r_ref.shape[1]
    wide = layers * rank
    d = lax.axis_index("dp")
    t = lax.axis_index("tensor")
    core = lax.rem(t, 2)
    place = lax.div(t, 2)
    partner = t + 1 - 2 * core
    n_y = n_t // 2
    half = width // 2
    piece = half // n_d
    block_rows = width // BLOCKS
    pair = 2 * own
    pack = own // layers
    tail = TAIL
    main = own - tail

    def remote(src, dst, send, recv, where):
        return pltpu.make_async_remote_copy(
            src_ref=src, dst_ref=dst, send_sem=send, recv_sem=recv, device_id=where, device_id_type=MESH
        )

    my_rows = pl.ds(pl.multiple_of(core * own, own), own)
    partner_rows = pl.ds(pl.multiple_of((1 - core) * own, own), own)

    barrier = pltpu.get_barrier_semaphore()
    for k in range(1, n_t):
        there = lax.rem(t + k, n_t)

        @pl.when(lax.rem(there, 2) == 0)
        def _():
            pl.semaphore_signal(barrier, inc=1, device_id={"tensor": there}, device_id_type=MESH)

    r_load = pltpu.make_async_copy(r_hbm, r_ref, local_sems.at[0])
    x_load = pltpu.make_async_copy(x_hbm, x_ref, local_sems.at[1])
    y_load = pltpu.make_async_copy(y_hbm, y_chip.at[:, my_rows, :], local_sems.at[2])
    e_loads = []
    for side in range(2):
        at = pl.ds(side * half, half)
        for layer in range(layers):
            e_loads.append(
                pltpu.make_async_copy(e_hbm.at[layer, at, :], m_ref.at[layer, at, :], e_sems.at[side, layer])
            )
    with jax.named_scope("bar"):

        @pl.when(core == 0)
        def _():
            pl.semaphore_wait(barrier, n_t - 1)
            pl.semaphore_signal(go_tensor, inc=1, device_id={"tensor": partner}, device_id_type=MESH)

        @pl.when(core == 1)
        def _():
            pl.semaphore_wait(go_tensor, 1)
            for k in range(1, n_d):
                pl.semaphore_signal(barrier, inc=1, device_id={"dp": lax.rem(d + k, n_d)}, device_id_type=MESH)

    chunks = []
    for layer in range(layers):
        row = 0
        while row < own:
            count = ROWS if layer < layers - 1 or row < main else LAST_ROWS
            chunks.append((layer, row, count))
            row += count
    total_chunks = len(chunks)

    def landing(i, m, side):
        layer, row, count = chunks[i]
        if layer == layers - 1 and row >= main:
            return yt_ref.at[m - 1, side, pl.ds(row - main, count), :]
        return y_far.at[layer, m - 1, side, pl.ds(row, count), :]

    def chunk_copy(i, m):
        layer, row, count = chunks[i]
        return remote(
            y_hbm.at[layer, pl.ds(row, count), :],
            landing(i, m, core),
            y_send.at[m - 1],
            y_recv.at[m - 1, i],
            {"tensor": lax.rem(t + 2 * m, n_t)},
        )

    middle = own // 2
    groups = [(layer, 0, own) for layer in range(layers - 1)]
    groups += [(layers - 1, 0, middle), (layers - 1, middle, main), (layers - 1, main, own)]

    def group_of(i):
        layer, row, _ = chunks[i]
        return [k for k, g in enumerate(groups) if g[0] == layer and g[1] <= row < g[2]][0]

    def forward_copy(i, m):
        here = landing(i, m, core)
        return remote(here, here, f_send.at[m - 1], f_recv.at[m - 1, group_of(i)], {"tensor": partner})

    def group_in(k, m):
        layer, start, stop = groups[k]
        if k == len(groups) - 1:
            here = yt_ref.at[m - 1, 1 - core]
        else:
            here = y_far.at[layer, m - 1, 1 - core, pl.ds(start, stop - start), :]
        return remote(here, here, f_send.at[m - 1], f_recv.at[m - 1, k], {"tensor": partner})

    sent = [0]
    passed = [0]

    def send_chunks(count):
        stop = min(sent[0] + count, total_chunks)
        for i in range(sent[0], stop):
            for m in range(1, n_y):
                chunk_copy(i, m).start()
        sent[0] = stop

    def pass_chunks(upto):
        for i in range(passed[0], min(upto, sent[0])):
            for m in range(1, n_y):
                chunk_copy(i, m).wait_recv()
                forward_copy(i, m).start()
        passed[0] = max(passed[0], min(upto, sent[0]))

    def need_group(k):
        for i in range(total_chunks):
            if group_of(i) <= k:
                pass_chunks(i + 1)
        for m in range(1, n_y):
            group_in(k, m).wait_recv()

    send_chunks(PLAN[0])
    own_copy = remote(y_hbm, y_chip.at[:, my_rows, :], own_sems.at[0], own_sems.at[1], {"tensor": partner})
    own_in = remote(y_hbm, y_chip.at[:, partner_rows, :], own_sems.at[0], own_sems.at[1], {"tensor": partner})

    r_load.start()
    x_load.start()
    def far_place(m):
        return lax.rem(place + n_y - m, n_y)

    r_load.wait()
    x_load.wait()
    for load in e_loads:
        load.start()
    y_load.start()
    r_parts = []
    for layer in range(layers):
        high, low = split(r_ref[layer])
        r_parts.append(jnp.concatenate([high, low] if layer % 2 == 0 else [low, high], axis=0))
    with jax.named_scope("token_terms"):
        for side in range(2):
            for other in range(n_y):
                at = pl.ds((2 * other + side) * own, own)
                parts = [dot(x_ref[layer, at, :], r_parts[layer], ((1,), (1,))) for layer in range(layers)]
                pt[side, other] = fold(parts, rank)
    pc_copy = remote(pt.at[1 - core], pt_core, pc_sems.at[0], pc_sems.at[1], {"tensor": partner})
    pc_copy.start()
    pc_copy.wait()
    p_total = None
    for m in range(1, n_y):
        there = lax.rem(place + m, n_y)
        pt_send[m - 1] = (pt[core, there] + pt_core[there]).astype(WIRE)
    p_out = []
    for m in range(1, n_y):
        copy = remote(
            pt_send.at[m - 1], pt_in.at[m - 1], p_send.at[m - 1], p_recv.at[m - 1], {"tensor": lax.rem(t + 2 * m, n_t)}
        )
        copy.start()
        p_out.append(copy)
    send_chunks(PLAN[1])
    p_total = pt[core, place] + pt_core[place]

    with jax.named_scope("left_of_error"):
        for side in range(2):
            for load in e_loads[side * layers : (side + 1) * layers]:
                load.wait()

            def left_of_error(i, carry):
                at = pl.ds(pl.multiple_of(side * half + i * block_rows, block_rows), block_rows)
                parts = [dot(m_ref[layer, at, :], r_parts[layer], ((1,), (1,))) for layer in range(layers)]
                lt[at, :] = fold(parts, rank)
                return carry

            lax.fori_loop(0, BLOCKS // 2, left_of_error, 0)
    y_load.wait()
    own_copy.start()
    with jax.named_scope("token_wait"):
        for copy in p_out:
            copy.wait()
    for m in range(1, n_y):
        p_total = p_total + pt_in[m - 1].astype(F32)
    p_high = p_total.astype(BF16).astype(F32)
    p_low = p_total - p_high
    if layers == 2:
        first = lax.broadcasted_iota(jnp.int32, (1, wide), 1) < rank
        turned = pltpu.roll(p_low, rank, 1)
        p_parts = [jnp.where(first, p_high, turned).astype(BF16), jnp.where(first, turned, p_high).astype(BF16)]
    else:
        p_parts = [
            jnp.concatenate([part[:, k * rank : (k + 1) * rank] for part in (p_high, p_low)], axis=1).astype(BF16)
            for k in range(layers)
        ]

    mine = pl.multiple_of(core * half, half)
    other = pl.multiple_of((1 - core) * half, half)

    def left_of_tokens(start):
        def step(i, carry):
            at = pl.ds(pl.multiple_of(start + i * block_rows, block_rows), block_rows)
            parts = [dot(y_chip[layer, my_rows, at], p_parts[layer], ((0,), (0,))) for layer in range(layers)]
            lt[at, :] += fold(parts, rank)
            return carry

        lax.fori_loop(0, BLOCKS // 2, step, 0)

    core_copy = remote(lt.at[pl.ds(other, half), :], lt_core, c_sems.at[0], c_sems.at[1], {"tensor": partner})
    with jax.named_scope("left_of_tokens"):
        left_of_tokens(other)
        core_copy.start()
        left_of_tokens(mine)
    with jax.named_scope("core_wait"):
        core_copy.wait()

    def add_core(j, carry):
        at = pl.ds(pl.multiple_of(mine + j * piece, piece), piece)
        value = lt[at, :] + lt_core[pl.ds(pl.multiple_of(j * piece, piece), piece), :]
        lt_send[j] = value.astype(lt_send.dtype)
        return carry

    lax.fori_loop(0, n_d, add_core, 0)
    with jax.named_scope("bar_dp"):

        @pl.when(core == 1)
        def _():
            pl.semaphore_wait(barrier, n_d - 1)
            pl.semaphore_signal(go_dp, inc=1, device_id={"tensor": partner}, device_id_type=MESH)

        @pl.when(core == 0)
        def _():
            pl.semaphore_wait(go_dp, 1)

    next_d = {"dp": lax.rem(d + 1, n_d)}
    for k in range(1, n_d):
        there = lax.rem(d + k, n_d)
        remote(lt_send.at[there], lt_in.at[k - 1], d_sems.at[0], d_sems.at[1], {"dp": there}).start()
    send_chunks(PLAN[2])

    def moment_of_chip(layer):
        tokens_here = pl.ds(pl.multiple_of(place * pair, pair), pair)

        def step(i, carry):
            at = pl.ds(pl.multiple_of(i * block_rows, block_rows), block_rows)
            term = dot(y_chip[layer, :, at], x_ref[layer, tokens_here, :], ((0,), (0,)))
            m_ref[layer, at, :] = (m_ref[layer, at, :].astype(F32) + term).astype(BF16)
            return carry

        with jax.named_scope("moment"):
            lax.fori_loop(0, BLOCKS, step, 0)

    def low_rank(at, layer):
        basis = ltf[at, :]
        return dot(jnp.concatenate([basis, basis], axis=1), t_err[layer], ((1,), (0,)))

    def add_far(layer, start, stop, with_rank):
        def step(i, carry):
            at = pl.ds(pl.multiple_of(i * block_rows, block_rows), block_rows)
            value = m_ref[layer, at, :].astype(F32)
            if with_rank:
                value = value + low_rank(at, layer)
            for m in range(1, n_y):
                base = far_place(m) * pair
                if stop == start:
                    continue
                y_rows = [y_far[layer, m - 1, side, start:stop, at] for side in range(2)]
                x_rows = [
                    x_ref[layer, pl.ds(pl.multiple_of(base + side * own + start, 16), stop - start), :]
                    for side in range(2)
                ]
                value = value + dot(jnp.concatenate(y_rows, axis=0), jnp.concatenate(x_rows, axis=0), ((0,), (0,)))
            m_ref[layer, at, :] = value.astype(BF16)
            return carry

        with jax.named_scope("far_terms"):
            lax.fori_loop(0, BLOCKS, step, 0)

    own_in.wait_recv()
    moment_of_chip(0)
    with jax.named_scope("dp_wait"):
        remote(lt_in, lt_in, d_sems.at[0], d_sems.at[1], next_d).wait()
    total = lt_send[d].astype(F32)
    for k in range(n_d - 1):
        total = total + lt_in[k].astype(F32)
    lt_sum[...] = total
    s_out = []
    for m in range(1, n_y):
        copy = remote(lt_sum, lt_y.at[m - 1], s_send.at[m - 1], s_recv.at[m - 1], {"tensor": lax.rem(t + 2 * m, n_t)})
        copy.start()
        s_out.append(copy)
    send_chunks(PLAN[3])
    pass_chunks(PASSED)
    with jax.named_scope("sum_wait"):
        for copy in s_out:
            copy.wait()
    total = lt_sum[...]
    for m in range(n_y - 1):
        total = total + lt_y[m]

    def slot(side, index):
        return ltf.at[pl.ds(pl.multiple_of(side * half + index * piece, piece), piece), :]

    ltf[pl.ds(pl.multiple_of(mine + d * piece, piece), piece), :] = total.astype(ltf.dtype)
    for k in range(1, n_d):
        there = lax.rem(d + k, n_d)
        remote(slot(core, d), slot(core, d), g_send, g_recv.at[k - 1], {"dp": there}).start()
    for layer in range(1, layers):
        moment_of_chip(layer)
    for k in range(layers - 1):
        need_group(k)
        add_far(k, 0, own, False)
    with jax.named_scope("gather_wait"):
        for k in range(n_d):
            source = lax.rem(d + n_d - k, n_d)
            if k > 0:
                remote(
                    slot(core, source), slot(core, source), g_send, g_recv.at[k - 1], {"dp": source}
                ).wait_recv()
            remote(slot(core, source), slot(core, source), h_sems.at[0], h_sems.at[1], {"tensor": partner}).start()
        here = ltf.at[pl.ds(other, half), :]
        remote(here, here, h_sems.at[0], h_sems.at[1], {"tensor": partner}).wait()

    slots_out = ltf.at[pl.ds(0, (n_d - 1) * piece), :]
    lanes = lax.broadcasted_iota(jnp.int32, (1, wide), 1) // rank
    sublanes = lax.broadcasted_iota(jnp.int32, (wide, 1), 0) // rank

    def merge(parts, index):
        value = parts[0]
        for layer in range(1, layers):
            value = jnp.where(index == layer, parts[layer], value)
        return value

    with jax.named_scope("token_right"):
        terms = dot(y_chip[layers - 1, my_rows, :], ltf[...], ((1,), (0,)))
        packed = []
        for k in range(layers):
            part = terms[k * pack : (k + 1) * pack]
            packed.append(part if k == layers - 1 else pltpu.roll(part, (k + 1) * rank, 1))
        q_own[...] = merge(packed, lanes).astype(q_own.dtype)
    q_out = []
    for m in range(1, n_y):
        copy = remote(
            q_own, q_far.at[m - 1, core], q_send.at[m - 1], q_recv.at[m - 1], {"tensor": lax.rem(t + 2 * m, n_t)}
        )
        copy.start()
        q_out.append(copy)
    send_chunks(total_chunks)
    with jax.named_scope("right_of_chip"):
        right = merge([dot(ltf[...], m_ref[layer], ((0,), (0,))) for layer in range(layers)], sublanes)
    with jax.named_scope("token_right_wait"):
        q_pass = []
        for m in range(1, n_y):
            here = q_far.at[m - 1, core]
            remote(q_own, here, q_send.at[m - 1], q_recv.at[m - 1], {"tensor": lax.rem(t + 2 * m, n_t)}).wait_recv()
            copy = remote(here, here, qf_send.at[m - 1], qf_recv.at[m - 1], {"tensor": partner})
            copy.start()
            q_pass.append(copy)
        for m in range(1, n_y):
            here = q_far.at[m - 1, 1 - core]
            remote(here, here, qf_send.at[m - 1], qf_recv.at[m - 1], {"tensor": partner}).wait_recv()
    far_right = jnp.zeros((rank, feats), F32)
    for m in range(1, n_y):
        basis = q_far[m - 1].reshape(2 * pack, wide)
        for k in range(layers):
            rows = [
                x_ref[layers - 1, pl.ds(pl.multiple_of(far_place(m) * pair + side * own + k * pack, 16), pack), :]
                for side in range(2)
            ]
            term = dot(basis, jnp.concatenate(rows, axis=0), ((0,), (0,)))
            far_right = far_right + term[k * rank : (k + 1) * rank]
    right = jnp.concatenate([right[: wide - rank], right[wide - rank :] + far_right], axis=0)
    share = wide // n_d
    for j in range(n_d):
        r_send[j] = right[j * share : (j + 1) * share, :].astype(BF16)
    for k in range(1, n_d):
        there = lax.rem(d + k, n_d)
        remote(r_send.at[there], r_in.at[k - 1], a_sems.at[0], a_sems.at[1], {"dp": there}).start()

    with jax.named_scope("inverse"):
        gram = dot(ltf[...], ltf[...], ((0,), (0,)))
        grams = [gram[k * rank : (k + 1) * rank, k * rank : (k + 1) * rank] for k in range(layers)]
        inverses = [
            lax.dot_general(
                factor, factor, (((0,), (0,)), ((), ())), precision=HIGHEST, preferred_element_type=F32
            )
            for factor in inverse_factors(grams)
        ]
    with jax.named_scope("right_wait"):
        remote(r_in, r_in, a_sems.at[0], a_sems.at[1], next_d).wait()
    total = r_send[d].astype(F32)
    for k in range(n_d - 1):
        total = total + r_in[k].astype(F32)
    r_all[n_d - 1] = total.astype(BF16)
    for k in range(1, n_d):
        there = lax.rem(d + k, n_d)
        remote(r_all.at[n_d - 1], r_all.at[k - 1], b_sems.at[0], b_sems.at[1], {"dp": there}).start()
    need_group(len(groups) - 3)
    add_far(layers - 1, 0, middle, False)
    with jax.named_scope("right_gather_wait"):
        gathered = r_all.at[pl.ds(0, n_d - 1)]
        remote(gathered, gathered, b_sems.at[0], b_sems.at[1], next_d).wait()
    for source in range(n_d):
        s_all[source * share : (source + 1) * share, :] = r_all[lax.rem(d + n_d - 1 - source, n_d)].astype(F32)
    t_err[...] = jnp.zeros_like(t_err)
    for layer in range(layers):
        rows = pl.ds(layer * rank, rank)
        scaled = lax.dot_general(
            inverses[layer],
            s_all[layer * rank : (layer + 1) * rank, :],
            (((1,), (0,)), ((), ())),
            precision=HIGHEST,
            preferred_element_type=F32,
        )
        high, low = split(scaled * (-1.0 / n_d))
        t_err[layer, layer * rank : (layer + 1) * rank, :] = high
        t_err[layer, wide + layer * rank : wide + (layer + 1) * rank, :] = low

    for layer in range(layers):
        add_far(layer, 0, 0, True)
    own_rows = width // n_d
    for layer in range(layers):
        value = low_rank(pl.ds(pl.multiple_of(d * own_rows, own_rows), own_rows), layer)
        sum_ref[layer] = (value * (-1.0 * n_d)).astype(sum_ref.dtype)
    for m in range(1, n_y):
        for side in range(2):
            rows = pl.ds(pl.multiple_of(far_place(m) * pair + side * own + main, 16), tail)
            xt_ref[m - 1, side] = x_ref[layers - 1, rows, :]
    with jax.named_scope("far_wait"):
        need_group(len(groups) - 2)
    add_far(layers - 1, middle, main, False)
    own_copy.wait_send()
    remote(slots_out, slots_out, g_send, h_sems.at[1], next_d).wait_send()
    for copy in q_out + q_pass:
        copy.wait_send()
    with jax.named_scope("tail_wait"):
        need_group(len(groups) - 1)
    whole = y_chip.at[:, my_rows, :]
    for m in range(1, n_y):
        remote(whole, whole, y_send.at[m - 1], y_recv.at[m - 1, 0], next_d).wait_send()
        remote(whole, whole, f_send.at[m - 1], f_recv.at[m - 1, 0], next_d).wait_send()


def finish_kernel(m_ref, sum_ref, yt_ref, xt_ref, err_hbm, out_hbm, stage, m_sems, sum_sem, block_sems):
    layers, width, feats = m_ref.shape
    block_rows = width // BLOCKS
    copies = [pltpu.make_async_copy(m_ref.at[layer], err_hbm.at[layer], m_sems.at[layer]) for layer in range(layers - 1)]
    copies.append(pltpu.make_async_copy(sum_ref, out_hbm, sum_sem))
    for copy in copies:
        copy.start()
    rows = xt_ref.shape[0] * xt_ref.shape[1] * xt_ref.shape[2]
    x_rows = xt_ref[...].reshape(rows, feats)
    for i in range(BLOCKS):
        at = pl.ds(i * block_rows, block_rows)
        term = dot(yt_ref[:, :, :, at].reshape(rows, block_rows), x_rows, ((0,), (0,)))
        stage[at, :] = (m_ref[layers - 1, at, :].astype(F32) + term).astype(stage.dtype)
        copy = pltpu.make_async_copy(stage.at[at, :], err_hbm.at[layers - 1, at, :], block_sems.at[i])
        copy.start()
        copies.append(copy)
    for copy in copies:
        copy.wait()


def solution(mesh):
    n_d, n_t = mesh.shape["dp"], mesh.shape["tensor"]

    def body(context, out_grad, error_in, right_init):
        layers, tokens, feats = context.shape
        own, width = out_grad.shape[1:]
        rank = right_init.shape[1]
        wide = layers * rank
        half = width // 2
        piece = half // n_d
        share = wide // n_d
        n_y = n_t // 2
        far = max(n_y - 1, 1)
        n_c = layers * (own // LAST_ROWS)
        rows = width // n_d
        dma = pltpu.SemaphoreType.DMA
        any_spec = pl.BlockSpec(memory_space=pl.ANY)
        vmem_spec = pl.BlockSpec(memory_space=pltpu.VMEM)
        pairs = lambda *shape: [dma(shape), dma(shape)]
        moment, summed, y_tail, x_tail = pl.pallas_call(
            functools.partial(comm_kernel, n_d, n_t),
            name="low_rank_chain",
            out_shape=(
                pltpu.VMEM((layers, width, feats), BF16),
                pltpu.VMEM((layers, rows, feats), BF16),
                pltpu.VMEM((far, 2, TAIL, width), BF16),
                pltpu.VMEM((far, 2, TAIL, feats), BF16),
            ),
            in_specs=[any_spec] * 4,
            out_specs=(vmem_spec,) * 4,
            scratch_shapes=[
                pltpu.VMEM((layers, tokens, feats), BF16),
                pltpu.VMEM((layers, 2 * own, width), BF16),
                pltpu.VMEM((layers, far, 2, own, width), BF16),
                pltpu.VMEM((layers, rank, feats), F32),
                pltpu.VMEM((2, n_y, own, wide), F32),
                pltpu.VMEM((n_y, own, wide), F32),
                pltpu.VMEM((far, own, wide), WIRE),
                pltpu.VMEM((far, own, wide), WIRE),
                pltpu.VMEM((own // layers, wide), WIRE),
                pltpu.VMEM((far, 2, own // layers, wide), WIRE),
                pltpu.VMEM((width, wide), F32),
                pltpu.VMEM((half, wide), F32),
                pltpu.VMEM((n_d, piece, wide), WIRE),
                pltpu.VMEM((n_d - 1, piece, wide), WIRE),
                pltpu.VMEM((far, piece, wide), F32),
                pltpu.VMEM((piece, wide), F32),
                pltpu.VMEM((width, wide), WIRE),
                pltpu.VMEM((n_d, share, feats), BF16),
                pltpu.VMEM((n_d - 1, share, feats), BF16),
                pltpu.VMEM((n_d, share, feats), BF16),
                pltpu.VMEM((wide, feats), F32),
                pltpu.VMEM((layers, 2 * wide, feats), BF16),
                dma((3,)),
                dma((2, layers)),
            ]
            + [dma((far,)), dma((far, n_c)), dma((far,)), dma((far, layers + 2)), dma((2,))]
            + pairs(far)
            + [dma((2,)), dma((2,)), dma((2,))]
            + pairs(far)
            + [dma, dma((n_d - 1,)), dma((2,))]
            + pairs(far)
            + pairs(far)
            + [dma((2,)), dma((2,))]
            + [pltpu.SemaphoreType.REGULAR, pltpu.SemaphoreType.REGULAR],
            compiler_params=pltpu.CompilerParams(
                collective_id=0, has_side_effects=True, vmem_limit_bytes=40 * 1024 * 1024
            ),
        )(*(pltpu.with_memory_space_constraint(a, pltpu.HBM) for a in (context, out_grad, error_in, right_init)))
        new_error, total = pl.pallas_call(
            finish_kernel,
            name="new_error",
            in_specs=[vmem_spec] * 4,
            out_specs=(any_spec, any_spec),
            out_shape=(
                jax.ShapeDtypeStruct((layers, width, feats), BF16),
                jax.ShapeDtypeStruct((layers, rows, feats), BF16),
            ),
            scratch_shapes=[pltpu.VMEM((width, feats), BF16), dma((layers,)), dma, dma((BLOCKS,))],
            compiler_params=pltpu.CompilerParams(vmem_limit_bytes=16 * 1024 * 1024),
        )(moment, summed, y_tail, x_tail)
        return total, new_error

    return jax.shard_map(
        body,
        mesh=mesh,
        in_specs=(
            P(None, "dp", "tensor"),
            P(None, ("dp", "tensor"), None),
            P(None, "dp", "tensor"),
            P(None, None, "tensor"),
        ),
        out_specs=(P(None, "dp", "tensor"), P(None, "dp", "tensor")),
        check_vma=False,
    )
```

```python
import functools

import jax
import jax.numpy as jnp
from jax import lax
from jax.experimental import pallas as pl
from jax.experimental.pallas import tpu as pltpu
from jax.sharding import PartitionSpec as P

MESH = pl.DeviceIdType.MESH
HIGHEST = lax.Precision.HIGHEST
F32 = jnp.float32
BF16 = jnp.bfloat16
WIRE = jnp.bfloat16
ROWS = 16
LAST_ROWS = 16
TAIL = 32
PASSED = 9
BLOCKS = 6
PLAN = (3, 6, 4, 8)


def split(value):
    high = value.astype(BF16)
    return high, (value - high.astype(F32)).astype(BF16)


def dot(a, b, dims):
    return lax.dot_general(a, b, (dims, ((), ())), preferred_element_type=F32)


def inverse_factors(grams):
    size = grams[0].shape[0]
    rows = lax.broadcasted_iota(jnp.int32, (size, size), 0)
    cols = lax.broadcasted_iota(jnp.int32, (size, size), 1)
    eye = (rows == cols).astype(F32)
    wide_rows = lax.broadcasted_iota(jnp.int32, (size, 2 * size), 0)
    work = []
    for gram in grams:
        mean = jnp.sum(jnp.sum(gram * eye, axis=1, keepdims=True), axis=0, keepdims=True) / size
        work.append(jnp.concatenate([gram + (1e-06 * mean) * eye, eye], axis=1))
    scales = [jnp.zeros((size, 1), F32) for _ in grams]
    one_col = wide_rows[:, :1]
    for k in range(size):
        for i, full in enumerate(work):
            row = full[k : k + 1, :]
            pivot = full[k : k + 1, k : k + 1]
            ratio = jnp.where(one_col > k, full[:, k : k + 1] / pivot, 0.0)
            scales[i] = jnp.where(one_col == k, lax.rsqrt(pivot), scales[i])
            work[i] = full - ratio * row
    return [full[:, size:] * scale for full, scale in zip(work, scales)]


def fold(parts, rank):
    if len(parts) == 2:
        first = lax.broadcasted_iota(jnp.int32, (1, 2 * rank), 1) < rank
        kept = jnp.where(first, parts[0], parts[1])
        moved = jnp.where(first, parts[1], parts[0])
        return kept + pltpu.roll(moved, rank, 1)
    return jnp.concatenate([part[:, :rank] + part[:, rank:] for part in parts], axis=1)


def comm_kernel(
    n_d,
    n_t,
    x_hbm,
    y_hbm,
    e_hbm,
    r_hbm,
    m_ref,
    sum_ref,
    yt_ref,
    xt_ref,
    x_ref,
    y_chip,
    y_far,
    r_ref,
    pt,
    pt_core,
    pt_send,
    pt_in,
    q_own,
    q_far,
    lt,
    lt_core,
    lt_send,
    lt_in,
    lt_y,
    ltf,
    r_send,
    r_in,
    r_all,
    s_all,
    t_err,
    local_sems,
    e_sems,
    y_send,
    y_recv,
    f_send,
    f_recv,
    own_sems,
    p_send,
    p_recv,
    pc_sems,
    c_sems,
    d_sems,
    s_send,
    s_recv,
    g_send,
    g_recv,
    h_sems,
    q_send,
    q_recv,
    qf_send,
    qf_recv,
    a_sems,
    b_sems,
    go_tensor,
    go_dp,
):
    layers, own, width = y_hbm.shape
    tokens, feats = x_ref.shape[1:]
    rank = r_ref.shape[1]
    wide = layers * rank
    d = lax.axis_index("dp")
    t = lax.axis_index("tensor")
    core = lax.rem(t, 2)
    place = lax.div(t, 2)
    partner = t + 1 - 2 * core
    n_y = n_t // 2
    half = width // 2
    piece = half // n_d
    block_rows = width // BLOCKS
    pair = 2 * own
    pack = own // layers
    tail = TAIL
    main = own - tail

    def remote(src, dst, send, recv, where):
        return pltpu.make_async_remote_copy(
            src_ref=src, dst_ref=dst, send_sem=send, recv_sem=recv, device_id=where, device_id_type=MESH
        )

    my_rows = pl.ds(pl.multiple_of(core * own, own), own)
    partner_rows = pl.ds(pl.multiple_of((1 - core) * own, own), own)

    barrier = pltpu.get_barrier_semaphore()
    for k in range(1, n_t):
        there = lax.rem(t + k, n_t)

        @pl.when(lax.rem(there, 2) == 0)
        def _():
            pl.semaphore_signal(barrier, inc=1, device_id={"tensor": there}, device_id_type=MESH)

    r_load = pltpu.make_async_copy(r_hbm, r_ref, local_sems.at[0])
    x_load = pltpu.make_async_copy(x_hbm, x_ref, local_sems.at[1])
    y_load = pltpu.make_async_copy(y_hbm, y_chip.at[:, my_rows, :], local_sems.at[2])
    e_loads = []
    for side in range(2):
        at = pl.ds(side * half, half)
        for layer in range(layers):
            e_loads.append(
                pltpu.make_async_copy(e_hbm.at[layer, at, :], m_ref.at[layer, at, :], e_sems.at[side, layer])
            )
    with jax.named_scope("bar"):

        @pl.when(core == 0)
        def _():
            pl.semaphore_wait(barrier, n_t - 1)
            pl.semaphore_signal(go_tensor, inc=1, device_id={"tensor": partner}, device_id_type=MESH)

        @pl.when(core == 1)
        def _():
            pl.semaphore_wait(go_tensor, 1)
            for k in range(1, n_d):
                pl.semaphore_signal(barrier, inc=1, device_id={"dp": lax.rem(d + k, n_d)}, device_id_type=MESH)

    chunks = []
    for layer in range(layers):
        row = 0
        while row < own:
            count = ROWS if layer < layers - 1 or row < main else LAST_ROWS
            chunks.append((layer, row, count))
            row += count
    total_chunks = len(chunks)

    def landing(i, m, side):
        layer, row, count = chunks[i]
        if layer == layers - 1 and row >= main:
            return yt_ref.at[m - 1, side, pl.ds(row - main, count), :]
        return y_far.at[layer, m - 1, side, pl.ds(row, count), :]

    def chunk_copy(i, m):
        layer, row, count = chunks[i]
        return remote(
            y_hbm.at[layer, pl.ds(row, count), :],
            landing(i, m, core),
            y_send.at[m - 1],
            y_recv.at[m - 1, i],
            {"tensor": lax.rem(t + 2 * m, n_t)},
        )

    middle = own // 2
    groups = [(layer, 0, own) for layer in range(layers - 1)]
    groups += [(layers - 1, 0, middle), (layers - 1, middle, main), (layers - 1, main, own)]

    def group_of(i):
        layer, row, _ = chunks[i]
        return [k for k, g in enumerate(groups) if g[0] == layer and g[1] <= row < g[2]][0]

    def forward_copy(i, m):
        here = landing(i, m, core)
        return remote(here, here, f_send.at[m - 1], f_recv.at[m - 1, group_of(i)], {"tensor": partner})

    def group_in(k, m):
        layer, start, stop = groups[k]
        if k == len(groups) - 1:
            here = yt_ref.at[m - 1, 1 - core]
        else:
            here = y_far.at[layer, m - 1, 1 - core, pl.ds(start, stop - start), :]
        return remote(here, here, f_send.at[m - 1], f_recv.at[m - 1, k], {"tensor": partner})

    sent = [0]
    passed = [0]

    def send_chunks(count):
        stop = min(sent[0] + count, total_chunks)
        for i in range(sent[0], stop):
            for m in range(1, n_y):
                chunk_copy(i, m).start()
        sent[0] = stop

    def pass_chunks(upto):
        for i in range(passed[0], min(upto, sent[0])):
            for m in range(1, n_y):
                chunk_copy(i, m).wait_recv()
                forward_copy(i, m).start()
        passed[0] = max(passed[0], min(upto, sent[0]))

    def need_group(k):
        for i in range(total_chunks):
            if group_of(i) <= k:
                pass_chunks(i + 1)
        for m in range(1, n_y):
            group_in(k, m).wait_recv()

    send_chunks(PLAN[0])
    own_copy = remote(y_hbm, y_chip.at[:, my_rows, :], own_sems.at[0], own_sems.at[1], {"tensor": partner})
    own_in = remote(y_hbm, y_chip.at[:, partner_rows, :], own_sems.at[0], own_sems.at[1], {"tensor": partner})

    r_load.start()
    x_load.start()
    def far_place(m):
        return lax.rem(place + n_y - m, n_y)

    r_load.wait()
    x_load.wait()
    for load in e_loads:
        load.start()
    y_load.start()
    r_parts = []
    for layer in range(layers):
        high, low = split(r_ref[layer])
        r_parts.append(jnp.concatenate([high, low] if layer % 2 == 0 else [low, high], axis=0))
    with jax.named_scope("token_terms"):
        for side in range(2):
            for other in range(n_y):
                at = pl.ds((2 * other + side) * own, own)
                parts = [dot(x_ref[layer, at, :], r_parts[layer], ((1,), (1,))) for layer in range(layers)]
                pt[side, other] = fold(parts, rank)
    pc_copy = remote(pt.at[1 - core], pt_core, pc_sems.at[0], pc_sems.at[1], {"tensor": partner})
    pc_copy.start()
    pc_copy.wait()
    p_total = None
    for m in range(1, n_y):
        there = lax.rem(place + m, n_y)
        pt_send[m - 1] = (pt[core, there] + pt_core[there]).astype(WIRE)
    p_out = []
    for m in range(1, n_y):
        copy = remote(
            pt_send.at[m - 1], pt_in.at[m - 1], p_send.at[m - 1], p_recv.at[m - 1], {"tensor": lax.rem(t + 2 * m, n_t)}
        )
        copy.start()
        p_out.append(copy)
    send_chunks(PLAN[1])
    p_total = pt[core, place] + pt_core[place]

    with jax.named_scope("left_of_error"):
        for side in range(2):
            for load in e_loads[side * layers : (side + 1) * layers]:
                load.wait()

            def left_of_error(i, carry):
                at = pl.ds(pl.multiple_of(side * half + i * block_rows, block_rows), block_rows)
                parts = [dot(m_ref[layer, at, :], r_parts[layer], ((1,), (1,))) for layer in range(layers)]
                lt[at, :] = fold(parts, rank)
                return carry

            lax.fori_loop(0, BLOCKS // 2, left_of_error, 0)
    y_load.wait()
    own_copy.start()
    with jax.named_scope("token_wait"):
        for copy in p_out:
            copy.wait()
    for m in range(1, n_y):
        p_total = p_total + pt_in[m - 1].astype(F32)
    p_high = p_total.astype(BF16).astype(F32)
    p_low = p_total - p_high
    if layers == 2:
        first = lax.broadcasted_iota(jnp.int32, (1, wide), 1) < rank
        turned = pltpu.roll(p_low, rank, 1)
        p_parts = [jnp.where(first, p_high, turned).astype(BF16), jnp.where(first, turned, p_high).astype(BF16)]
    else:
        p_parts = [
            jnp.concatenate([part[:, k * rank : (k + 1) * rank] for part in (p_high, p_low)], axis=1).astype(BF16)
            for k in range(layers)
        ]

    mine = pl.multiple_of(core * half, half)
    other = pl.multiple_of((1 - core) * half, half)

    def left_of_tokens(start):
        def step(i, carry):
            at = pl.ds(pl.multiple_of(start + i * block_rows, block_rows), block_rows)
            parts = [dot(y_chip[layer, my_rows, at], p_parts[layer], ((0,), (0,))) for layer in range(layers)]
            lt[at, :] += fold(parts, rank)
            return carry

        lax.fori_loop(0, BLOCKS // 2, step, 0)

    core_copy = remote(lt.at[pl.ds(other, half), :], lt_core, c_sems.at[0], c_sems.at[1], {"tensor": partner})
    with jax.named_scope("left_of_tokens"):
        left_of_tokens(other)
        core_copy.start()
        left_of_tokens(mine)
    with jax.named_scope("core_wait"):
        core_copy.wait()

    def add_core(j, carry):
        at = pl.ds(pl.multiple_of(mine + j * piece, piece), piece)
        value = lt[at, :] + lt_core[pl.ds(pl.multiple_of(j * piece, piece), piece), :]
        lt_send[j] = value.astype(lt_send.dtype)
        return carry

    lax.fori_loop(0, n_d, add_core, 0)
    with jax.named_scope("bar_dp"):

        @pl.when(core == 1)
        def _():
            pl.semaphore_wait(barrier, n_d - 1)
            pl.semaphore_signal(go_dp, inc=1, device_id={"tensor": partner}, device_id_type=MESH)

        @pl.when(core == 0)
        def _():
            pl.semaphore_wait(go_dp, 1)

    next_d = {"dp": lax.rem(d + 1, n_d)}
    for k in range(1, n_d):
        there = lax.rem(d + k, n_d)
        remote(lt_send.at[there], lt_in.at[k - 1], d_sems.at[0], d_sems.at[1], {"dp": there}).start()
    send_chunks(PLAN[2])

    def moment_of_chip(layer):
        tokens_here = pl.ds(pl.multiple_of(place * pair, pair), pair)

        def step(i, carry):
            at = pl.ds(pl.multiple_of(i * block_rows, block_rows), block_rows)
            term = dot(y_chip[layer, :, at], x_ref[layer, tokens_here, :], ((0,), (0,)))
            m_ref[layer, at, :] = (m_ref[layer, at, :].astype(F32) + term).astype(BF16)
            return carry

        with jax.named_scope("moment"):
            lax.fori_loop(0, BLOCKS, step, 0)

    def low_rank(at, layer):
        basis = ltf[at, :]
        return dot(jnp.concatenate([basis, basis], axis=1), t_err[layer], ((1,), (0,)))

    def add_far(layer, start, stop, with_rank):
        def step(i, carry):
            at = pl.ds(pl.multiple_of(i * block_rows, block_rows), block_rows)
            value = m_ref[layer, at, :].astype(F32)
            if with_rank:
                value = value + low_rank(at, layer)
            for m in range(1, n_y):
                base = far_place(m) * pair
                if stop == start:
                    continue
                y_rows = [y_far[layer, m - 1, side, start:stop, at] for side in range(2)]
                x_rows = [
                    x_ref[layer, pl.ds(pl.multiple_of(base + side * own + start, 16), stop - start), :]
                    for side in range(2)
                ]
                value = value + dot(jnp.concatenate(y_rows, axis=0), jnp.concatenate(x_rows, axis=0), ((0,), (0,)))
            m_ref[layer, at, :] = value.astype(BF16)
            return carry

        with jax.named_scope("far_terms"):
            lax.fori_loop(0, BLOCKS, step, 0)

    own_in.wait_recv()
    moment_of_chip(0)
    with jax.named_scope("dp_wait"):
        remote(lt_in, lt_in, d_sems.at[0], d_sems.at[1], next_d).wait()
    total = lt[pl.ds(pl.multiple_of(mine + d * piece, piece), piece), :]
    total = total + lt_core[pl.ds(pl.multiple_of(d * piece, piece), piece), :]
    for k in range(n_d - 1):
        total = total + lt_in[k].astype(F32)
    lt_y[n_y - 1] = total.astype(lt_y.dtype)
    s_out = []
    for m in range(1, n_y):
        copy = remote(lt_y.at[n_y - 1], lt_y.at[m - 1], s_send.at[m - 1], s_recv.at[m - 1], {"tensor": lax.rem(t + 2 * m, n_t)})
        copy.start()
        s_out.append(copy)
    send_chunks(PLAN[3])
    pass_chunks(PASSED)
    with jax.named_scope("sum_wait"):
        for copy in s_out:
            copy.wait()
    total = lt_y[lax.rem(place + n_y - 1, n_y)].astype(F32)
    for source in range(1, n_y):
        total = total + lt_y[lax.rem(place + 2 * n_y - 1 - source, n_y)].astype(F32)

    def slot(side, index):
        return ltf.at[pl.ds(pl.multiple_of(side * half + index * piece, piece), piece), :]

    ltf[pl.ds(pl.multiple_of(mine + d * piece, piece), piece), :] = total.astype(ltf.dtype)
    for k in range(1, n_d):
        there = lax.rem(d + k, n_d)
        remote(slot(core, d), slot(core, d), g_send, g_recv.at[k - 1], {"dp": there}).start()
    for layer in range(1, layers):
        moment_of_chip(layer)
    for k in range(layers - 1):
        need_group(k)
        add_far(k, 0, own, False)
    with jax.named_scope("gather_wait"):
        for k in range(n_d):
            source = lax.rem(d + n_d - k, n_d)
            if k > 0:
                remote(
                    slot(core, source), slot(core, source), g_send, g_recv.at[k - 1], {"dp": source}
                ).wait_recv()
            remote(slot(core, source), slot(core, source), h_sems.at[0], h_sems.at[1], {"tensor": partner}).start()
        here = ltf.at[pl.ds(other, half), :]
        remote(here, here, h_sems.at[0], h_sems.at[1], {"tensor": partner}).wait()

    slots_out = ltf.at[pl.ds(0, (n_d - 1) * piece), :]
    lanes = lax.broadcasted_iota(jnp.int32, (1, wide), 1) // rank
    sublanes = lax.broadcasted_iota(jnp.int32, (wide, 1), 0) // rank

    def merge(parts, index):
        value = parts[0]
        for layer in range(1, layers):
            value = jnp.where(index == layer, parts[layer], value)
        return value

    with jax.named_scope("token_right"):
        terms = dot(y_chip[layers - 1, my_rows, :], ltf[...], ((1,), (0,)))
        packed = []
        for k in range(layers):
            part = terms[k * pack : (k + 1) * pack]
            packed.append(part if k == layers - 1 else pltpu.roll(part, (k + 1) * rank, 1))
        q_own[...] = merge(packed, lanes).astype(q_own.dtype)
    q_out = []
    for m in range(1, n_y):
        copy = remote(
            q_own, q_far.at[m - 1, core], q_send.at[m - 1], q_recv.at[m - 1], {"tensor": lax.rem(t + 2 * m, n_t)}
        )
        copy.start()
        q_out.append(copy)
    send_chunks(total_chunks)
    with jax.named_scope("right_of_chip"):
        right = merge([dot(ltf[...], m_ref[layer], ((0,), (0,))) for layer in range(layers)], sublanes)
    with jax.named_scope("token_right_wait"):
        q_pass = []
        for m in range(1, n_y):
            here = q_far.at[m - 1, core]
            remote(q_own, here, q_send.at[m - 1], q_recv.at[m - 1], {"tensor": lax.rem(t + 2 * m, n_t)}).wait_recv()
            copy = remote(here, here, qf_send.at[m - 1], qf_recv.at[m - 1], {"tensor": partner})
            copy.start()
            q_pass.append(copy)
        for m in range(1, n_y):
            here = q_far.at[m - 1, 1 - core]
            remote(here, here, qf_send.at[m - 1], qf_recv.at[m - 1], {"tensor": partner}).wait_recv()
    far_right = jnp.zeros((rank, feats), F32)
    for m in range(1, n_y):
        basis = q_far[m - 1].reshape(2 * pack, wide)
        for k in range(layers):
            rows = [
                x_ref[layers - 1, pl.ds(pl.multiple_of(far_place(m) * pair + side * own + k * pack, 16), pack), :]
                for side in range(2)
            ]
            term = dot(basis, jnp.concatenate(rows, axis=0), ((0,), (0,)))
            far_right = far_right + term[k * rank : (k + 1) * rank]
    right = jnp.concatenate([right[: wide - rank], right[wide - rank :] + far_right], axis=0)
    share = wide // n_d
    for j in range(n_d):
        r_send[j] = right[j * share : (j + 1) * share, :].astype(BF16)
    for k in range(1, n_d):
        there = lax.rem(d + k, n_d)
        remote(r_send.at[there], r_in.at[k - 1], a_sems.at[0], a_sems.at[1], {"dp": there}).start()

    with jax.named_scope("inverse"):
        gram = dot(ltf[...], ltf[...], ((0,), (0,)))
        grams = [gram[k * rank : (k + 1) * rank, k * rank : (k + 1) * rank] for k in range(layers)]
        inverses = [
            lax.dot_general(
                factor, factor, (((0,), (0,)), ((), ())), precision=HIGHEST, preferred_element_type=F32
            )
            for factor in inverse_factors(grams)
        ]
    with jax.named_scope("right_wait"):
        remote(r_in, r_in, a_sems.at[0], a_sems.at[1], next_d).wait()
    total = r_send[d].astype(F32)
    for k in range(n_d - 1):
        total = total + r_in[k].astype(F32)
    r_all[n_d - 1] = total.astype(BF16)
    for k in range(1, n_d):
        there = lax.rem(d + k, n_d)
        remote(r_all.at[n_d - 1], r_all.at[k - 1], b_sems.at[0], b_sems.at[1], {"dp": there}).start()
    need_group(len(groups) - 3)
    add_far(layers - 1, 0, middle, False)
    with jax.named_scope("right_gather_wait"):
        gathered = r_all.at[pl.ds(0, n_d - 1)]
        remote(gathered, gathered, b_sems.at[0], b_sems.at[1], next_d).wait()
    for source in range(n_d):
        s_all[source * share : (source + 1) * share, :] = r_all[lax.rem(d + n_d - 1 - source, n_d)].astype(F32)
    t_err[...] = jnp.zeros_like(t_err)
    for layer in range(layers):
        rows = pl.ds(layer * rank, rank)
        scaled = lax.dot_general(
            inverses[layer],
            s_all[layer * rank : (layer + 1) * rank, :],
            (((1,), (0,)), ((), ())),
            precision=HIGHEST,
            preferred_element_type=F32,
        )
        high, low = split(scaled * (-1.0 / n_d))
        t_err[layer, layer * rank : (layer + 1) * rank, :] = high
        t_err[layer, wide + layer * rank : wide + (layer + 1) * rank, :] = low

    for layer in range(layers):
        add_far(layer, 0, 0, True)
    own_rows = width // n_d
    for layer in range(layers):
        value = low_rank(pl.ds(pl.multiple_of(d * own_rows, own_rows), own_rows), layer)
        sum_ref[layer] = (value * (-1.0 * n_d)).astype(sum_ref.dtype)
    for m in range(1, n_y):
        for side in range(2):
            rows = pl.ds(pl.multiple_of(far_place(m) * pair + side * own + main, 16), tail)
            xt_ref[m - 1, side] = x_ref[layers - 1, rows, :]
    with jax.named_scope("far_wait"):
        need_group(len(groups) - 2)
    add_far(layers - 1, middle, main, False)
    own_copy.wait_send()
    remote(slots_out, slots_out, g_send, h_sems.at[1], next_d).wait_send()
    for copy in q_out + q_pass:
        copy.wait_send()
    with jax.named_scope("tail_wait"):
        need_group(len(groups) - 1)
    whole = y_chip.at[:, my_rows, :]
    for m in range(1, n_y):
        remote(whole, whole, y_send.at[m - 1], y_recv.at[m - 1, 0], next_d).wait_send()
        remote(whole, whole, f_send.at[m - 1], f_recv.at[m - 1, 0], next_d).wait_send()


def finish_kernel(m_ref, sum_ref, yt_ref, xt_ref, err_hbm, out_hbm, stage, m_sems, sum_sem, block_sems):
    layers, width, feats = m_ref.shape
    block_rows = width // BLOCKS
    copies = [pltpu.make_async_copy(m_ref.at[layer], err_hbm.at[layer], m_sems.at[layer]) for layer in range(layers - 1)]
    copies.append(pltpu.make_async_copy(sum_ref, out_hbm, sum_sem))
    for copy in copies:
        copy.start()
    rows = xt_ref.shape[0] * xt_ref.shape[1] * xt_ref.shape[2]
    x_rows = xt_ref[...].reshape(rows, feats)
    for i in range(BLOCKS):
        at = pl.ds(i * block_rows, block_rows)
        term = dot(yt_ref[:, :, :, at].reshape(rows, block_rows), x_rows, ((0,), (0,)))
        stage[at, :] = (m_ref[layers - 1, at, :].astype(F32) + term).astype(stage.dtype)
        copy = pltpu.make_async_copy(stage.at[at, :], err_hbm.at[layers - 1, at, :], block_sems.at[i])
        copy.start()
        copies.append(copy)
    for copy in copies:
        copy.wait()


def solution(mesh):
    n_d, n_t = mesh.shape["dp"], mesh.shape["tensor"]

    def body(context, out_grad, error_in, right_init):
        layers, tokens, feats = context.shape
        own, width = out_grad.shape[1:]
        rank = right_init.shape[1]
        wide = layers * rank
        half = width // 2
        piece = half // n_d
        share = wide // n_d
        n_y = n_t // 2
        far = max(n_y - 1, 1)
        n_c = layers * (own // LAST_ROWS)
        rows = width // n_d
        dma = pltpu.SemaphoreType.DMA
        any_spec = pl.BlockSpec(memory_space=pl.ANY)
        vmem_spec = pl.BlockSpec(memory_space=pltpu.VMEM)
        pairs = lambda *shape: [dma(shape), dma(shape)]
        moment, summed, y_tail, x_tail = pl.pallas_call(
            functools.partial(comm_kernel, n_d, n_t),
            name="low_rank_chain",
            out_shape=(
                pltpu.VMEM((layers, width, feats), BF16),
                pltpu.VMEM((layers, rows, feats), BF16),
                pltpu.VMEM((far, 2, TAIL, width), BF16),
                pltpu.VMEM((far, 2, TAIL, feats), BF16),
            ),
            in_specs=[any_spec] * 4,
            out_specs=(vmem_spec,) * 4,
            scratch_shapes=[
                pltpu.VMEM((layers, tokens, feats), BF16),
                pltpu.VMEM((layers, 2 * own, width), BF16),
                pltpu.VMEM((layers, far, 2, own, width), BF16),
                pltpu.VMEM((layers, rank, feats), F32),
                pltpu.VMEM((2, n_y, own, wide), F32),
                pltpu.VMEM((n_y, own, wide), F32),
                pltpu.VMEM((far, own, wide), WIRE),
                pltpu.VMEM((far, own, wide), WIRE),
                pltpu.VMEM((own // layers, wide), WIRE),
                pltpu.VMEM((far, 2, own // layers, wide), WIRE),
                pltpu.VMEM((width, wide), F32),
                pltpu.VMEM((half, wide), F32),
                pltpu.VMEM((n_d, piece, wide), WIRE),
                pltpu.VMEM((n_d - 1, piece, wide), WIRE),
                pltpu.VMEM((n_y, piece, wide), WIRE),
                pltpu.VMEM((width, wide), WIRE),
                pltpu.VMEM((n_d, share, feats), BF16),
                pltpu.VMEM((n_d - 1, share, feats), BF16),
                pltpu.VMEM((n_d, share, feats), BF16),
                pltpu.VMEM((wide, feats), F32),
                pltpu.VMEM((layers, 2 * wide, feats), BF16),
                dma((3,)),
                dma((2, layers)),
            ]
            + [dma((far,)), dma((far, n_c)), dma((far,)), dma((far, layers + 2)), dma((2,))]
            + pairs(far)
            + [dma((2,)), dma((2,)), dma((2,))]
            + pairs(far)
            + [dma, dma((n_d - 1,)), dma((2,))]
            + pairs(far)
            + pairs(far)
            + [dma((2,)), dma((2,))]
            + [pltpu.SemaphoreType.REGULAR, pltpu.SemaphoreType.REGULAR],
            compiler_params=pltpu.CompilerParams(
                collective_id=0, has_side_effects=True, vmem_limit_bytes=40 * 1024 * 1024
            ),
        )(*(pltpu.with_memory_space_constraint(a, pltpu.HBM) for a in (context, out_grad, error_in, right_init)))
        new_error, total = pl.pallas_call(
            finish_kernel,
            name="new_error",
            in_specs=[vmem_spec] * 4,
            out_specs=(any_spec, any_spec),
            out_shape=(
                jax.ShapeDtypeStruct((layers, width, feats), BF16),
                jax.ShapeDtypeStruct((layers, rows, feats), BF16),
            ),
            scratch_shapes=[pltpu.VMEM((width, feats), BF16), dma((layers,)), dma, dma((BLOCKS,))],
            compiler_params=pltpu.CompilerParams(vmem_limit_bytes=16 * 1024 * 1024),
        )(moment, summed, y_tail, x_tail)
        return total, new_error

    return jax.shard_map(
        body,
        mesh=mesh,
        in_specs=(
            P(None, "dp", "tensor"),
            P(None, ("dp", "tensor"), None),
            P(None, "dp", "tensor"),
            P(None, None, "tensor"),
        ),
        out_specs=(P(None, "dp", "tensor"), P(None, "dp", "tensor")),
        check_vma=False,
    )
```

```python
import functools

import jax
import jax.numpy as jnp
from jax import lax
from jax.experimental import pallas as pl
from jax.experimental.pallas import tpu as pltpu
from jax.sharding import PartitionSpec as P

MESH = pl.DeviceIdType.MESH
HIGHEST = lax.Precision.HIGHEST
F32 = jnp.float32
BF16 = jnp.bfloat16
WIRE = jnp.bfloat16
ROWS = 16
LAST_ROWS = 16
TAIL = 32
PASSED = 9
PASS_LATE = 4
BLOCKS = 6
PLAN = (2, 7, 4, 8)


def split(value):
    high = value.astype(BF16)
    return high, (value - high.astype(F32)).astype(BF16)


def dot(a, b, dims):
    return lax.dot_general(a, b, (dims, ((), ())), preferred_element_type=F32)


def inverse_factors(grams):
    size = grams[0].shape[0]
    rows = lax.broadcasted_iota(jnp.int32, (size, size), 0)
    cols = lax.broadcasted_iota(jnp.int32, (size, size), 1)
    eye = (rows == cols).astype(F32)
    wide_rows = lax.broadcasted_iota(jnp.int32, (size, 2 * size), 0)
    work = []
    for gram in grams:
        mean = jnp.sum(jnp.sum(gram * eye, axis=1, keepdims=True), axis=0, keepdims=True) / size
        work.append(jnp.concatenate([gram + (1e-06 * mean) * eye, eye], axis=1))
    scales = [jnp.zeros((size, 1), F32) for _ in grams]
    one_col = wide_rows[:, :1]
    for k in range(size):
        for i, full in enumerate(work):
            row = full[k : k + 1, :]
            pivot = full[k : k + 1, k : k + 1]
            ratio = jnp.where(one_col > k, full[:, k : k + 1] / pivot, 0.0)
            scales[i] = jnp.where(one_col == k, lax.rsqrt(pivot), scales[i])
            work[i] = full - ratio * row
    return [full[:, size:] * scale for full, scale in zip(work, scales)]


def fold(parts, rank):
    if len(parts) == 2:
        first = lax.broadcasted_iota(jnp.int32, (1, 2 * rank), 1) < rank
        kept = jnp.where(first, parts[0], parts[1])
        moved = jnp.where(first, parts[1], parts[0])
        return kept + pltpu.roll(moved, rank, 1)
    return jnp.concatenate([part[:, :rank] + part[:, rank:] for part in parts], axis=1)


def comm_kernel(
    n_d,
    n_t,
    x_hbm,
    y_hbm,
    e_hbm,
    r_hbm,
    m_ref,
    sum_ref,
    yt_ref,
    xt_ref,
    x_ref,
    y_chip,
    y_far,
    r_ref,
    pt,
    pt_core,
    pt_send,
    pt_in,
    q_own,
    q_far,
    lt,
    lt_core,
    lt_send,
    lt_in,
    lt_y,
    ltf,
    r_send,
    r_in,
    r_all,
    s_all,
    t_err,
    local_sems,
    e_sems,
    y_send,
    y_recv,
    f_send,
    f_recv,
    own_sems,
    p_send,
    p_recv,
    pc_sems,
    c_sems,
    d_sems,
    s_send,
    s_recv,
    g_send,
    g_recv,
    h_sems,
    q_send,
    q_recv,
    qf_send,
    qf_recv,
    a_sems,
    b_sems,
    go_tensor,
    go_dp,
):
    layers, own, width = y_hbm.shape
    tokens, feats = x_ref.shape[1:]
    rank = r_ref.shape[1]
    wide = layers * rank
    d = lax.axis_index("dp")
    t = lax.axis_index("tensor")
    core = lax.rem(t, 2)
    place = lax.div(t, 2)
    partner = t + 1 - 2 * core
    n_y = n_t // 2
    half = width // 2
    piece = half // n_d
    block_rows = width // BLOCKS
    pair = 2 * own
    pack = own // layers
    tail = TAIL
    main = own - tail

    def remote(src, dst, send, recv, where):
        return pltpu.make_async_remote_copy(
            src_ref=src, dst_ref=dst, send_sem=send, recv_sem=recv, device_id=where, device_id_type=MESH
        )

    my_rows = pl.ds(pl.multiple_of(core * own, own), own)
    partner_rows = pl.ds(pl.multiple_of((1 - core) * own, own), own)

    barrier = pltpu.get_barrier_semaphore()
    for k in range(1, n_t):
        there = lax.rem(t + k, n_t)

        @pl.when(lax.rem(there, 2) == 0)
        def _():
            pl.semaphore_signal(barrier, inc=1, device_id={"tensor": there}, device_id_type=MESH)

    r_load = pltpu.make_async_copy(r_hbm, r_ref, local_sems.at[0])
    x_load = pltpu.make_async_copy(x_hbm, x_ref, local_sems.at[1])
    y_load = pltpu.make_async_copy(y_hbm, y_chip.at[:, my_rows, :], local_sems.at[2])
    e_loads = []
    for side in range(2):
        at = pl.ds(side * half, half)
        for layer in range(layers):
            e_loads.append(
                pltpu.make_async_copy(e_hbm.at[layer, at, :], m_ref.at[layer, at, :], e_sems.at[side, layer])
            )
    with jax.named_scope("bar"):

        @pl.when(core == 0)
        def _():
            pl.semaphore_wait(barrier, n_t - 1)
            pl.semaphore_signal(go_tensor, inc=1, device_id={"tensor": partner}, device_id_type=MESH)

        @pl.when(core == 1)
        def _():
            pl.semaphore_wait(go_tensor, 1)
            for k in range(1, n_d):
                pl.semaphore_signal(barrier, inc=1, device_id={"dp": lax.rem(d + k, n_d)}, device_id_type=MESH)

    chunks = []
    for layer in range(layers):
        row = 0
        while row < own:
            count = ROWS if layer < layers - 1 or row < main else LAST_ROWS
            chunks.append((layer, row, count))
            row += count
    total_chunks = len(chunks)

    def landing(i, m, side):
        layer, row, count = chunks[i]
        if layer == layers - 1 and row >= main:
            return yt_ref.at[m - 1, side, pl.ds(row - main, count), :]
        return y_far.at[layer, m - 1, side, pl.ds(row, count), :]

    def chunk_copy(i, m):
        layer, row, count = chunks[i]
        return remote(
            y_hbm.at[layer, pl.ds(row, count), :],
            landing(i, m, core),
            y_send.at[m - 1],
            y_recv.at[m - 1, i],
            {"tensor": lax.rem(t + 2 * m, n_t)},
        )

    middle = own // 2
    groups = [(layer, 0, own) for layer in range(layers - 1)]
    groups += [(layers - 1, 0, middle), (layers - 1, middle, main), (layers - 1, main, own)]

    def group_of(i):
        layer, row, _ = chunks[i]
        return [k for k, g in enumerate(groups) if g[0] == layer and g[1] <= row < g[2]][0]

    def forward_copy(i, m):
        here = landing(i, m, core)
        return remote(here, here, f_send.at[m - 1], f_recv.at[m - 1, group_of(i)], {"tensor": partner})

    def group_in(k, m):
        layer, start, stop = groups[k]
        if k == len(groups) - 1:
            here = yt_ref.at[m - 1, 1 - core]
        else:
            here = y_far.at[layer, m - 1, 1 - core, pl.ds(start, stop - start), :]
        return remote(here, here, f_send.at[m - 1], f_recv.at[m - 1, k], {"tensor": partner})

    sent = [0]
    passed = [0]

    def send_chunks(count):
        stop = min(sent[0] + count, total_chunks)
        for i in range(sent[0], stop):
            for m in range(1, n_y):
                chunk_copy(i, m).start()
        sent[0] = stop

    def pass_chunks(upto):
        for i in range(passed[0], min(upto, sent[0])):
            for m in range(1, n_y):
                chunk_copy(i, m).wait_recv()
                forward_copy(i, m).start()
        passed[0] = max(passed[0], min(upto, sent[0]))

    def need_group(k):
        for i in range(total_chunks):
            if group_of(i) <= k:
                pass_chunks(i + 1)
        for m in range(1, n_y):
            group_in(k, m).wait_recv()

    send_chunks(PLAN[0])
    own_copy = remote(y_hbm, y_chip.at[:, my_rows, :], own_sems.at[0], own_sems.at[1], {"tensor": partner})
    own_in = remote(y_hbm, y_chip.at[:, partner_rows, :], own_sems.at[0], own_sems.at[1], {"tensor": partner})

    r_load.start()
    x_load.start()
    def far_place(m):
        return lax.rem(place + n_y - m, n_y)

    r_load.wait()
    x_load.wait()
    for load in e_loads:
        load.start()
    y_load.start()
    r_parts = []
    for layer in range(layers):
        high, low = split(r_ref[layer])
        r_parts.append(jnp.concatenate([high, low] if layer % 2 == 0 else [low, high], axis=0))
    with jax.named_scope("token_terms"):
        for side in range(2):
            for other in range(n_y):
                at = pl.ds((2 * other + side) * own, own)
                parts = [dot(x_ref[layer, at, :], r_parts[layer], ((1,), (1,))) for layer in range(layers)]
                pt[side, other] = fold(parts, rank)
    pc_copy = remote(pt.at[1 - core], pt_core, pc_sems.at[0], pc_sems.at[1], {"tensor": partner})
    pc_copy.start()
    pc_copy.wait()
    p_total = None
    for m in range(1, n_y):
        there = lax.rem(place + m, n_y)
        pt_send[m - 1] = (pt[core, there] + pt_core[there]).astype(WIRE)
    p_out = []
    for m in range(1, n_y):
        copy = remote(
            pt_send.at[m - 1], pt_in.at[m - 1], p_send.at[m - 1], p_recv.at[m - 1], {"tensor": lax.rem(t + 2 * m, n_t)}
        )
        copy.start()
        p_out.append(copy)
    send_chunks(PLAN[1])
    p_total = pt[core, place] + pt_core[place]

    with jax.named_scope("left_of_error"):
        for side in range(2):
            for load in e_loads[side * layers : (side + 1) * layers]:
                load.wait()

            def left_of_error(i, carry):
                at = pl.ds(pl.multiple_of(side * half + i * block_rows, block_rows), block_rows)
                parts = [dot(m_ref[layer, at, :], r_parts[layer], ((1,), (1,))) for layer in range(layers)]
                lt[at, :] = fold(parts, rank)
                return carry

            lax.fori_loop(0, BLOCKS // 2, left_of_error, 0)
    y_load.wait()
    own_copy.start()
    with jax.named_scope("token_wait"):
        for copy in p_out:
            copy.wait()
    for m in range(1, n_y):
        p_total = p_total + pt_in[m - 1].astype(F32)
    p_high = p_total.astype(BF16).astype(F32)
    p_low = p_total - p_high
    if layers == 2:
        first = lax.broadcasted_iota(jnp.int32, (1, wide), 1) < rank
        turned = pltpu.roll(p_low, rank, 1)
        p_parts = [jnp.where(first, p_high, turned).astype(BF16), jnp.where(first, turned, p_high).astype(BF16)]
    else:
        p_parts = [
            jnp.concatenate([part[:, k * rank : (k + 1) * rank] for part in (p_high, p_low)], axis=1).astype(BF16)
            for k in range(layers)
        ]

    mine = pl.multiple_of(core * half, half)
    other = pl.multiple_of((1 - core) * half, half)

    def left_of_tokens(start):
        def step(i, carry):
            at = pl.ds(pl.multiple_of(start + i * block_rows, block_rows), block_rows)
            parts = [dot(y_chip[layer, my_rows, at], p_parts[layer], ((0,), (0,))) for layer in range(layers)]
            lt[at, :] += fold(parts, rank)
            return carry

        lax.fori_loop(0, BLOCKS // 2, step, 0)

    core_copy = remote(lt.at[pl.ds(other, half), :], lt_core, c_sems.at[0], c_sems.at[1], {"tensor": partner})
    with jax.named_scope("left_of_tokens"):
        left_of_tokens(other)
        core_copy.start()
        left_of_tokens(mine)
    with jax.named_scope("core_wait"):
        core_copy.wait()

    def add_core(j, carry):
        at = pl.ds(pl.multiple_of(mine + j * piece, piece), piece)
        value = lt[at, :] + lt_core[pl.ds(pl.multiple_of(j * piece, piece), piece), :]
        lt_send[j] = value.astype(lt_send.dtype)
        return carry

    lax.fori_loop(0, n_d, add_core, 0)
    with jax.named_scope("bar_dp"):

        @pl.when(core == 1)
        def _():
            pl.semaphore_wait(barrier, n_d - 1)
            pl.semaphore_signal(go_dp, inc=1, device_id={"tensor": partner}, device_id_type=MESH)

        @pl.when(core == 0)
        def _():
            pl.semaphore_wait(go_dp, 1)

    next_d = {"dp": lax.rem(d + 1, n_d)}
    for k in range(1, n_d):
        there = lax.rem(d + k, n_d)
        remote(lt_send.at[there], lt_in.at[k - 1], d_sems.at[0], d_sems.at[1], {"dp": there}).start()
    send_chunks(PLAN[2])

    def moment_of_chip(layer):
        tokens_here = pl.ds(pl.multiple_of(place * pair, pair), pair)

        def step(i, carry):
            at = pl.ds(pl.multiple_of(i * block_rows, block_rows), block_rows)
            term = dot(y_chip[layer, :, at], x_ref[layer, tokens_here, :], ((0,), (0,)))
            m_ref[layer, at, :] = (m_ref[layer, at, :].astype(F32) + term).astype(BF16)
            return carry

        with jax.named_scope("moment"):
            lax.fori_loop(0, BLOCKS, step, 0)

    def low_rank(at, layer):
        basis = ltf[at, :]
        return dot(jnp.concatenate([basis, basis], axis=1), t_err[layer], ((1,), (0,)))

    def add_far(layer, start, stop, with_rank):
        def step(i, carry):
            at = pl.ds(pl.multiple_of(i * block_rows, block_rows), block_rows)
            value = m_ref[layer, at, :].astype(F32)
            if with_rank:
                value = value + low_rank(at, layer)
            for m in range(1, n_y):
                base = far_place(m) * pair
                if stop == start:
                    continue
                y_rows = [y_far[layer, m - 1, side, start:stop, at] for side in range(2)]
                x_rows = [
                    x_ref[layer, pl.ds(pl.multiple_of(base + side * own + start, 16), stop - start), :]
                    for side in range(2)
                ]
                value = value + dot(jnp.concatenate(y_rows, axis=0), jnp.concatenate(x_rows, axis=0), ((0,), (0,)))
            m_ref[layer, at, :] = value.astype(BF16)
            return carry

        with jax.named_scope("far_terms"):
            lax.fori_loop(0, BLOCKS, step, 0)

    own_in.wait_recv()
    moment_of_chip(0)
    with jax.named_scope("dp_wait"):
        remote(lt_in, lt_in, d_sems.at[0], d_sems.at[1], next_d).wait()
    total = lt[pl.ds(pl.multiple_of(mine + d * piece, piece), piece), :]
    total = total + lt_core[pl.ds(pl.multiple_of(d * piece, piece), piece), :]
    for k in range(n_d - 1):
        total = total + lt_in[k].astype(F32)
    lt_y[n_y - 1] = total.astype(lt_y.dtype)
    s_out = []
    for m in range(1, n_y):
        copy = remote(lt_y.at[n_y - 1], lt_y.at[m - 1], s_send.at[m - 1], s_recv.at[m - 1], {"tensor": lax.rem(t + 2 * m, n_t)})
        copy.start()
        s_out.append(copy)
    send_chunks(PLAN[3])
    pass_chunks(PASSED)
    with jax.named_scope("sum_wait"):
        for copy in s_out:
            copy.wait()
    total = lt_y[lax.rem(place + n_y - 1, n_y)].astype(F32)
    for source in range(1, n_y):
        total = total + lt_y[lax.rem(place + 2 * n_y - 1 - source, n_y)].astype(F32)

    def slot(side, index):
        return ltf.at[pl.ds(pl.multiple_of(side * half + index * piece, piece), piece), :]

    ltf[pl.ds(pl.multiple_of(mine + d * piece, piece), piece), :] = total.astype(ltf.dtype)
    for k in range(1, n_d):
        there = lax.rem(d + k, n_d)
        remote(slot(core, d), slot(core, d), g_send, g_recv.at[k - 1], {"dp": there}).start()
    for layer in range(1, layers):
        moment_of_chip(layer)
    for k in range(layers - 1):
        need_group(k)
        add_far(k, 0, own, False)
    with jax.named_scope("gather_wait"):
        for k in range(n_d):
            source = lax.rem(d + n_d - k, n_d)
            if k > 0:
                remote(
                    slot(core, source), slot(core, source), g_send, g_recv.at[k - 1], {"dp": source}
                ).wait_recv()
            remote(slot(core, source), slot(core, source), h_sems.at[0], h_sems.at[1], {"tensor": partner}).start()
        here = ltf.at[pl.ds(other, half), :]
        remote(here, here, h_sems.at[0], h_sems.at[1], {"tensor": partner}).wait()

    slots_out = ltf.at[pl.ds(0, (n_d - 1) * piece), :]
    lanes = lax.broadcasted_iota(jnp.int32, (1, wide), 1) // rank
    sublanes = lax.broadcasted_iota(jnp.int32, (wide, 1), 0) // rank

    def merge(parts, index):
        value = parts[0]
        for layer in range(1, layers):
            value = jnp.where(index == layer, parts[layer], value)
        return value

    with jax.named_scope("token_right"):
        terms = dot(y_chip[layers - 1, my_rows, :], ltf[...], ((1,), (0,)))
        packed = []
        for k in range(layers):
            part = terms[k * pack : (k + 1) * pack]
            packed.append(part if k == layers - 1 else pltpu.roll(part, (k + 1) * rank, 1))
        q_own[...] = merge(packed, lanes).astype(q_own.dtype)
    q_out = []
    for m in range(1, n_y):
        copy = remote(
            q_own, q_far.at[m - 1, core], q_send.at[m - 1], q_recv.at[m - 1], {"tensor": lax.rem(t + 2 * m, n_t)}
        )
        copy.start()
        q_out.append(copy)
    send_chunks(total_chunks)
    with jax.named_scope("right_of_chip"):
        right = merge([dot(ltf[...], m_ref[layer], ((0,), (0,))) for layer in range(layers)], sublanes)
    pass_chunks(sum(PLAN))
    with jax.named_scope("token_right_wait"):
        q_pass = []
        for m in range(1, n_y):
            here = q_far.at[m - 1, core]
            remote(q_own, here, q_send.at[m - 1], q_recv.at[m - 1], {"tensor": lax.rem(t + 2 * m, n_t)}).wait_recv()
            copy = remote(here, here, qf_send.at[m - 1], qf_recv.at[m - 1], {"tensor": partner})
            copy.start()
            q_pass.append(copy)
        for m in range(1, n_y):
            here = q_far.at[m - 1, 1 - core]
            remote(here, here, qf_send.at[m - 1], qf_recv.at[m - 1], {"tensor": partner}).wait_recv()
    far_right = jnp.zeros((rank, feats), F32)
    for m in range(1, n_y):
        basis = q_far[m - 1].reshape(2 * pack, wide)
        for k in range(layers):
            rows = [
                x_ref[layers - 1, pl.ds(pl.multiple_of(far_place(m) * pair + side * own + k * pack, 16), pack), :]
                for side in range(2)
            ]
            term = dot(basis, jnp.concatenate(rows, axis=0), ((0,), (0,)))
            far_right = far_right + term[k * rank : (k + 1) * rank]
    right = jnp.concatenate([right[: wide - rank], right[wide - rank :] + far_right], axis=0)
    share = wide // n_d
    for j in range(n_d):
        r_send[j] = right[j * share : (j + 1) * share, :].astype(BF16)
    for k in range(1, n_d):
        there = lax.rem(d + k, n_d)
        remote(r_send.at[there], r_in.at[k - 1], a_sems.at[0], a_sems.at[1], {"dp": there}).start()

    with jax.named_scope("inverse"):
        gram = dot(ltf[...], ltf[...], ((0,), (0,)))
        grams = [gram[k * rank : (k + 1) * rank, k * rank : (k + 1) * rank] for k in range(layers)]
        inverses = [
            lax.dot_general(
                factor, factor, (((0,), (0,)), ((), ())), precision=HIGHEST, preferred_element_type=F32
            )
            for factor in inverse_factors(grams)
        ]
    with jax.named_scope("right_wait"):
        remote(r_in, r_in, a_sems.at[0], a_sems.at[1], next_d).wait()
    total = r_send[d].astype(F32)
    for k in range(n_d - 1):
        total = total + r_in[k].astype(F32)
    r_all[n_d - 1] = total.astype(BF16)
    for k in range(1, n_d):
        there = lax.rem(d + k, n_d)
        remote(r_all.at[n_d - 1], r_all.at[k - 1], b_sems.at[0], b_sems.at[1], {"dp": there}).start()
    need_group(len(groups) - 3)
    add_far(layers - 1, 0, middle, False)
    with jax.named_scope("right_gather_wait"):
        gathered = r_all.at[pl.ds(0, n_d - 1)]
        remote(gathered, gathered, b_sems.at[0], b_sems.at[1], next_d).wait()
    for source in range(n_d):
        s_all[source * share : (source + 1) * share, :] = r_all[lax.rem(d + n_d - 1 - source, n_d)].astype(F32)
    t_err[...] = jnp.zeros_like(t_err)
    for layer in range(layers):
        rows = pl.ds(layer * rank, rank)
        scaled = lax.dot_general(
            inverses[layer],
            s_all[layer * rank : (layer + 1) * rank, :],
            (((1,), (0,)), ((), ())),
            precision=HIGHEST,
            preferred_element_type=F32,
        )
        high, low = split(scaled * (-1.0 / n_d))
        t_err[layer, layer * rank : (layer + 1) * rank, :] = high
        t_err[layer, wide + layer * rank : wide + (layer + 1) * rank, :] = low

    for layer in range(layers):
        pass_chunks(total_chunks - PASS_LATE + layer)
        add_far(layer, 0, 0, True)
    own_rows = width // n_d
    for layer in range(layers):
        value = low_rank(pl.ds(pl.multiple_of(d * own_rows, own_rows), own_rows), layer)
        sum_ref[layer] = (value * (-1.0 * n_d)).astype(sum_ref.dtype)
    for m in range(1, n_y):
        for side in range(2):
            rows = pl.ds(pl.multiple_of(far_place(m) * pair + side * own + main, 16), tail)
            xt_ref[m - 1, side] = x_ref[layers - 1, rows, :]
    with jax.named_scope("far_wait"):
        need_group(len(groups) - 2)
    add_far(layers - 1, middle, main, False)
    own_copy.wait_send()
    remote(slots_out, slots_out, g_send, h_sems.at[1], next_d).wait_send()
    for copy in q_out + q_pass:
        copy.wait_send()
    with jax.named_scope("tail_wait"):
        need_group(len(groups) - 1)
    whole = y_chip.at[:, my_rows, :]
    for m in range(1, n_y):
        remote(whole, whole, y_send.at[m - 1], y_recv.at[m - 1, 0], next_d).wait_send()
        remote(whole, whole, f_send.at[m - 1], f_recv.at[m - 1, 0], next_d).wait_send()


def finish_kernel(m_ref, sum_ref, yt_ref, xt_ref, err_hbm, out_hbm, stage, m_sems, sum_sem, block_sems):
    layers, width, feats = m_ref.shape
    block_rows = width // BLOCKS
    copies = [pltpu.make_async_copy(m_ref.at[layer], err_hbm.at[layer], m_sems.at[layer]) for layer in range(layers - 1)]
    copies.append(pltpu.make_async_copy(sum_ref, out_hbm, sum_sem))
    for copy in copies:
        copy.start()
    rows = xt_ref.shape[0] * xt_ref.shape[1] * xt_ref.shape[2]
    x_rows = xt_ref[...].reshape(rows, feats)
    for i in range(BLOCKS):
        at = pl.ds(i * block_rows, block_rows)
        term = dot(yt_ref[:, :, :, at].reshape(rows, block_rows), x_rows, ((0,), (0,)))
        stage[at, :] = (m_ref[layers - 1, at, :].astype(F32) + term).astype(stage.dtype)
        copy = pltpu.make_async_copy(stage.at[at, :], err_hbm.at[layers - 1, at, :], block_sems.at[i])
        copy.start()
        copies.append(copy)
    for copy in copies:
        copy.wait()


def solution(mesh):
    n_d, n_t = mesh.shape["dp"], mesh.shape["tensor"]

    def body(context, out_grad, error_in, right_init):
        layers, tokens, feats = context.shape
        own, width = out_grad.shape[1:]
        rank = right_init.shape[1]
        wide = layers * rank
        half = width // 2
        piece = half // n_d
        share = wide // n_d
        n_y = n_t // 2
        far = max(n_y - 1, 1)
        n_c = layers * (own // LAST_ROWS)
        rows = width // n_d
        dma = pltpu.SemaphoreType.DMA
        any_spec = pl.BlockSpec(memory_space=pl.ANY)
        vmem_spec = pl.BlockSpec(memory_space=pltpu.VMEM)
        pairs = lambda *shape: [dma(shape), dma(shape)]
        moment, summed, y_tail, x_tail = pl.pallas_call(
            functools.partial(comm_kernel, n_d, n_t),
            name="low_rank_chain",
            out_shape=(
                pltpu.VMEM((layers, width, feats), BF16),
                pltpu.VMEM((layers, rows, feats), BF16),
                pltpu.VMEM((far, 2, TAIL, width), BF16),
                pltpu.VMEM((far, 2, TAIL, feats), BF16),
            ),
            in_specs=[any_spec] * 4,
            out_specs=(vmem_spec,) * 4,
            scratch_shapes=[
                pltpu.VMEM((layers, tokens, feats), BF16),
                pltpu.VMEM((layers, 2 * own, width), BF16),
                pltpu.VMEM((layers, far, 2, own, width), BF16),
                pltpu.VMEM((layers, rank, feats), F32),
                pltpu.VMEM((2, n_y, own, wide), F32),
                pltpu.VMEM((n_y, own, wide), F32),
                pltpu.VMEM((far, own, wide), WIRE),
                pltpu.VMEM((far, own, wide), WIRE),
                pltpu.VMEM((own // layers, wide), WIRE),
                pltpu.VMEM((far, 2, own // layers, wide), WIRE),
                pltpu.VMEM((width, wide), F32),
                pltpu.VMEM((half, wide), F32),
                pltpu.VMEM((n_d, piece, wide), WIRE),
                pltpu.VMEM((n_d - 1, piece, wide), WIRE),
                pltpu.VMEM((n_y, piece, wide), WIRE),
                pltpu.VMEM((width, wide), WIRE),
                pltpu.VMEM((n_d, share, feats), BF16),
                pltpu.VMEM((n_d - 1, share, feats), BF16),
                pltpu.VMEM((n_d, share, feats), BF16),
                pltpu.VMEM((wide, feats), F32),
                pltpu.VMEM((layers, 2 * wide, feats), BF16),
                dma((3,)),
                dma((2, layers)),
            ]
            + [dma((far,)), dma((far, n_c)), dma((far,)), dma((far, layers + 2)), dma((2,))]
            + pairs(far)
            + [dma((2,)), dma((2,)), dma((2,))]
            + pairs(far)
            + [dma, dma((n_d - 1,)), dma((2,))]
            + pairs(far)
            + pairs(far)
            + [dma((2,)), dma((2,))]
            + [pltpu.SemaphoreType.REGULAR, pltpu.SemaphoreType.REGULAR],
            compiler_params=pltpu.CompilerParams(
                collective_id=0, has_side_effects=True, vmem_limit_bytes=40 * 1024 * 1024
            ),
        )(*(pltpu.with_memory_space_constraint(a, pltpu.HBM) for a in (context, out_grad, error_in, right_init)))
        new_error, total = pl.pallas_call(
            finish_kernel,
            name="new_error",
            in_specs=[vmem_spec] * 4,
            out_specs=(any_spec, any_spec),
            out_shape=(
                jax.ShapeDtypeStruct((layers, width, feats), BF16),
                jax.ShapeDtypeStruct((layers, rows, feats), BF16),
            ),
            scratch_shapes=[pltpu.VMEM((width, feats), BF16), dma((layers,)), dma, dma((BLOCKS,))],
            compiler_params=pltpu.CompilerParams(vmem_limit_bytes=16 * 1024 * 1024),
        )(moment, summed, y_tail, x_tail)
        return total, new_error

    return jax.shard_map(
        body,
        mesh=mesh,
        in_specs=(
            P(None, "dp", "tensor"),
            P(None, ("dp", "tensor"), None),
            P(None, "dp", "tensor"),
            P(None, None, "tensor"),
        ),
        out_specs=(P(None, "dp", "tensor"), P(None, "dp", "tensor")),
        check_vma=False,
    )
```

```python
import functools

import jax
import jax.numpy as jnp
from jax import lax
from jax.experimental import pallas as pl
from jax.experimental.pallas import tpu as pltpu
from jax.sharding import PartitionSpec as P

MESH = pl.DeviceIdType.MESH
HIGHEST = lax.Precision.HIGHEST
F32 = jnp.float32
BF16 = jnp.bfloat16
WIRE = jnp.bfloat16
ROWS = 16
LAST_ROWS = 16
TAIL = 48
PASSED = 9
PASS_LATE = 4
BLOCKS = 6
PLAN = (2, 7, 4, 8)


def split(value):
    high = value.astype(BF16)
    return high, (value - high.astype(F32)).astype(BF16)


def dot(a, b, dims):
    return lax.dot_general(a, b, (dims, ((), ())), preferred_element_type=F32)


def inverse_factors(grams):
    size = grams[0].shape[0]
    rows = lax.broadcasted_iota(jnp.int32, (size, size), 0)
    cols = lax.broadcasted_iota(jnp.int32, (size, size), 1)
    eye = (rows == cols).astype(F32)
    wide_rows = lax.broadcasted_iota(jnp.int32, (size, 2 * size), 0)
    work = []
    for gram in grams:
        mean = jnp.sum(jnp.sum(gram * eye, axis=1, keepdims=True), axis=0, keepdims=True) / size
        work.append(jnp.concatenate([gram + (1e-06 * mean) * eye, eye], axis=1))
    scales = [jnp.zeros((size, 1), F32) for _ in grams]
    one_col = wide_rows[:, :1]
    for k in range(size):
        for i, full in enumerate(work):
            row = full[k : k + 1, :]
            pivot = full[k : k + 1, k : k + 1]
            ratio = jnp.where(one_col > k, full[:, k : k + 1] / pivot, 0.0)
            scales[i] = jnp.where(one_col == k, lax.rsqrt(pivot), scales[i])
            work[i] = full - ratio * row
    return [full[:, size:] * scale for full, scale in zip(work, scales)]


def fold(parts, rank):
    if len(parts) == 2:
        first = lax.broadcasted_iota(jnp.int32, (1, 2 * rank), 1) < rank
        kept = jnp.where(first, parts[0], parts[1])
        moved = jnp.where(first, parts[1], parts[0])
        return kept + pltpu.roll(moved, rank, 1)
    return jnp.concatenate([part[:, :rank] + part[:, rank:] for part in parts], axis=1)


def comm_kernel(
    n_d,
    n_t,
    x_hbm,
    y_hbm,
    e_hbm,
    r_hbm,
    m_ref,
    sum_ref,
    yt_ref,
    xt_ref,
    x_ref,
    y_chip,
    y_far,
    r_ref,
    pt,
    pt_core,
    pt_send,
    pt_in,
    q_own,
    q_far,
    lt,
    lt_core,
    lt_send,
    lt_in,
    lt_y,
    ltf,
    r_send,
    r_in,
    r_all,
    s_all,
    t_err,
    local_sems,
    e_sems,
    y_send,
    y_recv,
    f_send,
    f_recv,
    own_sems,
    p_send,
    p_recv,
    pc_sems,
    c_sems,
    d_sems,
    s_send,
    s_recv,
    g_send,
    g_recv,
    h_sems,
    q_send,
    q_recv,
    qf_send,
    qf_recv,
    a_sems,
    b_sems,
    go_tensor,
    go_dp,
):
    layers, own, width = y_hbm.shape
    tokens, feats = x_ref.shape[1:]
    rank = r_ref.shape[1]
    wide = layers * rank
    d = lax.axis_index("dp")
    t = lax.axis_index("tensor")
    core = lax.rem(t, 2)
    place = lax.div(t, 2)
    partner = t + 1 - 2 * core
    n_y = n_t // 2
    half = width // 2
    piece = half // n_d
    block_rows = width // BLOCKS
    pair = 2 * own
    pack = own // layers
    tail = TAIL
    main = own - tail

    def remote(src, dst, send, recv, where):
        return pltpu.make_async_remote_copy(
            src_ref=src, dst_ref=dst, send_sem=send, recv_sem=recv, device_id=where, device_id_type=MESH
        )

    my_rows = pl.ds(pl.multiple_of(core * own, own), own)
    partner_rows = pl.ds(pl.multiple_of((1 - core) * own, own), own)

    barrier = pltpu.get_barrier_semaphore()
    for k in range(1, n_t):
        there = lax.rem(t + k, n_t)

        @pl.when(lax.rem(there, 2) == 0)
        def _():
            pl.semaphore_signal(barrier, inc=1, device_id={"tensor": there}, device_id_type=MESH)

    r_load = pltpu.make_async_copy(r_hbm, r_ref, local_sems.at[0])
    x_load = pltpu.make_async_copy(x_hbm, x_ref, local_sems.at[1])
    y_load = pltpu.make_async_copy(y_hbm, y_chip.at[:, my_rows, :], local_sems.at[2])
    e_loads = []
    for side in range(2):
        at = pl.ds(side * half, half)
        for layer in range(layers):
            e_loads.append(
                pltpu.make_async_copy(e_hbm.at[layer, at, :], m_ref.at[layer, at, :], e_sems.at[side, layer])
            )
    with jax.named_scope("bar"):

        @pl.when(core == 0)
        def _():
            pl.semaphore_wait(barrier, n_t - 1)
            pl.semaphore_signal(go_tensor, inc=1, device_id={"tensor": partner}, device_id_type=MESH)

        @pl.when(core == 1)
        def _():
            pl.semaphore_wait(go_tensor, 1)
            for k in range(1, n_d):
                pl.semaphore_signal(barrier, inc=1, device_id={"dp": lax.rem(d + k, n_d)}, device_id_type=MESH)

    chunks = []
    for layer in range(layers):
        row = 0
        while row < own:
            count = ROWS if layer < layers - 1 or row < main else LAST_ROWS
            chunks.append((layer, row, count))
            row += count
    total_chunks = len(chunks)

    def landing(i, m, side):
        layer, row, count = chunks[i]
        if layer == layers - 1 and row >= main:
            return yt_ref.at[m - 1, side, pl.ds(row - main, count), :]
        return y_far.at[layer, m - 1, side, pl.ds(row, count), :]

    def chunk_copy(i, m):
        layer, row, count = chunks[i]
        return remote(
            y_hbm.at[layer, pl.ds(row, count), :],
            landing(i, m, core),
            y_send.at[m - 1],
            y_recv.at[m - 1, i],
            {"tensor": lax.rem(t + 2 * m, n_t)},
        )

    middle = own // 2
    groups = [(layer, 0, own) for layer in range(layers - 1)]
    groups += [(layers - 1, 0, middle), (layers - 1, middle, main), (layers - 1, main, own)]

    def group_of(i):
        layer, row, _ = chunks[i]
        return [k for k, g in enumerate(groups) if g[0] == layer and g[1] <= row < g[2]][0]

    def forward_copy(i, m):
        here = landing(i, m, core)
        return remote(here, here, f_send.at[m - 1], f_recv.at[m - 1, group_of(i)], {"tensor": partner})

    def group_in(k, m):
        layer, start, stop = groups[k]
        if k == len(groups) - 1:
            here = yt_ref.at[m - 1, 1 - core]
        else:
            here = y_far.at[layer, m - 1, 1 - core, pl.ds(start, stop - start), :]
        return remote(here, here, f_send.at[m - 1], f_recv.at[m - 1, k], {"tensor": partner})

    sent = [0]
    passed = [0]

    def send_chunks(count):
        stop = min(sent[0] + count, total_chunks)
        for i in range(sent[0], stop):
            for m in range(1, n_y):
                chunk_copy(i, m).start()
        sent[0] = stop

    def pass_chunks(upto):
        for i in range(passed[0], min(upto, sent[0])):
            for m in range(1, n_y):
                chunk_copy(i, m).wait_recv()
                forward_copy(i, m).start()
        passed[0] = max(passed[0], min(upto, sent[0]))

    def need_group(k):
        for i in range(total_chunks):
            if group_of(i) <= k:
                pass_chunks(i + 1)
        for m in range(1, n_y):
            group_in(k, m).wait_recv()

    send_chunks(PLAN[0])
    own_copy = remote(y_hbm, y_chip.at[:, my_rows, :], own_sems.at[0], own_sems.at[1], {"tensor": partner})
    own_in = remote(y_hbm, y_chip.at[:, partner_rows, :], own_sems.at[0], own_sems.at[1], {"tensor": partner})

    r_load.start()
    x_load.start()
    def far_place(m):
        return lax.rem(place + n_y - m, n_y)

    r_load.wait()
    x_load.wait()
    for load in e_loads:
        load.start()
    y_load.start()
    r_parts = []
    for layer in range(layers):
        high, low = split(r_ref[layer])
        r_parts.append(jnp.concatenate([high, low] if layer % 2 == 0 else [low, high], axis=0))
    with jax.named_scope("token_terms"):
        for side in range(2):
            for other in range(n_y):
                at = pl.ds((2 * other + side) * own, own)
                parts = [dot(x_ref[layer, at, :], r_parts[layer], ((1,), (1,))) for layer in range(layers)]
                pt[side, other] = fold(parts, rank)
    pc_copy = remote(pt.at[1 - core], pt_core, pc_sems.at[0], pc_sems.at[1], {"tensor": partner})
    pc_copy.start()
    pc_copy.wait()
    p_total = None
    for m in range(1, n_y):
        there = lax.rem(place + m, n_y)
        pt_send[m - 1] = (pt[core, there] + pt_core[there]).astype(WIRE)
    p_out = []
    for m in range(1, n_y):
        copy = remote(
            pt_send.at[m - 1], pt_in.at[m - 1], p_send.at[m - 1], p_recv.at[m - 1], {"tensor": lax.rem(t + 2 * m, n_t)}
        )
        copy.start()
        p_out.append(copy)
    send_chunks(PLAN[1])
    p_total = pt[core, place] + pt_core[place]

    with jax.named_scope("left_of_error"):
        for side in range(2):
            for load in e_loads[side * layers : (side + 1) * layers]:
                load.wait()

            def left_of_error(i, carry):
                at = pl.ds(pl.multiple_of(side * half + i * block_rows, block_rows), block_rows)
                parts = [dot(m_ref[layer, at, :], r_parts[layer], ((1,), (1,))) for layer in range(layers)]
                lt[at, :] = fold(parts, rank)
                return carry

            lax.fori_loop(0, BLOCKS // 2, left_of_error, 0)
    y_load.wait()
    own_copy.start()
    with jax.named_scope("token_wait"):
        for copy in p_out:
            copy.wait()
    for m in range(1, n_y):
        p_total = p_total + pt_in[m - 1].astype(F32)
    p_high = p_total.astype(BF16).astype(F32)
    p_low = p_total - p_high
    if layers == 2:
        first = lax.broadcasted_iota(jnp.int32, (1, wide), 1) < rank
        turned = pltpu.roll(p_low, rank, 1)
        p_parts = [jnp.where(first, p_high, turned).astype(BF16), jnp.where(first, turned, p_high).astype(BF16)]
    else:
        p_parts = [
            jnp.concatenate([part[:, k * rank : (k + 1) * rank] for part in (p_high, p_low)], axis=1).astype(BF16)
            for k in range(layers)
        ]

    mine = pl.multiple_of(core * half, half)
    other = pl.multiple_of((1 - core) * half, half)

    def left_of_tokens(start):
        def step(i, carry):
            at = pl.ds(pl.multiple_of(start + i * block_rows, block_rows), block_rows)
            parts = [dot(y_chip[layer, my_rows, at], p_parts[layer], ((0,), (0,))) for layer in range(layers)]
            lt[at, :] += fold(parts, rank)
            return carry

        lax.fori_loop(0, BLOCKS // 2, step, 0)

    core_copy = remote(lt.at[pl.ds(other, half), :], lt_core, c_sems.at[0], c_sems.at[1], {"tensor": partner})
    with jax.named_scope("left_of_tokens"):
        left_of_tokens(other)
        core_copy.start()
        left_of_tokens(mine)
    with jax.named_scope("core_wait"):
        core_copy.wait()

    def add_core(j, carry):
        at = pl.ds(pl.multiple_of(mine + j * piece, piece), piece)
        value = lt[at, :] + lt_core[pl.ds(pl.multiple_of(j * piece, piece), piece), :]
        lt_send[j] = value.astype(lt_send.dtype)
        return carry

    lax.fori_loop(0, n_d, add_core, 0)
    with jax.named_scope("bar_dp"):

        @pl.when(core == 1)
        def _():
            pl.semaphore_wait(barrier, n_d - 1)
            pl.semaphore_signal(go_dp, inc=1, device_id={"tensor": partner}, device_id_type=MESH)

        @pl.when(core == 0)
        def _():
            pl.semaphore_wait(go_dp, 1)

    next_d = {"dp": lax.rem(d + 1, n_d)}
    for k in range(1, n_d):
        there = lax.rem(d + k, n_d)
        remote(lt_send.at[there], lt_in.at[k - 1], d_sems.at[0], d_sems.at[1], {"dp": there}).start()
    send_chunks(PLAN[2])

    def moment_of_chip(layer):
        tokens_here = pl.ds(pl.multiple_of(place * pair, pair), pair)

        def step(i, carry):
            at = pl.ds(pl.multiple_of(i * block_rows, block_rows), block_rows)
            term = dot(y_chip[layer, :, at], x_ref[layer, tokens_here, :], ((0,), (0,)))
            m_ref[layer, at, :] = (m_ref[layer, at, :].astype(F32) + term).astype(BF16)
            return carry

        with jax.named_scope("moment"):
            lax.fori_loop(0, BLOCKS, step, 0)

    def low_rank(at, layer):
        basis = ltf[at, :]
        return dot(jnp.concatenate([basis, basis], axis=1), t_err[layer], ((1,), (0,)))

    def add_far(layer, start, stop, with_rank):
        def step(i, carry):
            at = pl.ds(pl.multiple_of(i * block_rows, block_rows), block_rows)
            value = m_ref[layer, at, :].astype(F32)
            if with_rank:
                value = value + low_rank(at, layer)
            for m in range(1, n_y):
                base = far_place(m) * pair
                if stop == start:
                    continue
                y_rows = [y_far[layer, m - 1, side, start:stop, at] for side in range(2)]
                x_rows = [
                    x_ref[layer, pl.ds(pl.multiple_of(base + side * own + start, 16), stop - start), :]
                    for side in range(2)
                ]
                value = value + dot(jnp.concatenate(y_rows, axis=0), jnp.concatenate(x_rows, axis=0), ((0,), (0,)))
            m_ref[layer, at, :] = value.astype(BF16)
            return carry

        with jax.named_scope("far_terms"):
            lax.fori_loop(0, BLOCKS, step, 0)

    own_in.wait_recv()
    moment_of_chip(0)
    with jax.named_scope("dp_wait"):
        remote(lt_in, lt_in, d_sems.at[0], d_sems.at[1], next_d).wait()
    total = lt[pl.ds(pl.multiple_of(mine + d * piece, piece), piece), :]
    total = total + lt_core[pl.ds(pl.multiple_of(d * piece, piece), piece), :]
    for k in range(n_d - 1):
        total = total + lt_in[k].astype(F32)
    lt_y[n_y - 1] = total.astype(lt_y.dtype)
    s_out = []
    for m in range(1, n_y):
        copy = remote(lt_y.at[n_y - 1], lt_y.at[m - 1], s_send.at[m - 1], s_recv.at[m - 1], {"tensor": lax.rem(t + 2 * m, n_t)})
        copy.start()
        s_out.append(copy)
    send_chunks(PLAN[3])
    pass_chunks(PASSED)
    with jax.named_scope("sum_wait"):
        for copy in s_out:
            copy.wait()
    total = lt_y[lax.rem(place + n_y - 1, n_y)].astype(F32)
    for source in range(1, n_y):
        total = total + lt_y[lax.rem(place + 2 * n_y - 1 - source, n_y)].astype(F32)

    def slot(side, index):
        return ltf.at[pl.ds(pl.multiple_of(side * half + index * piece, piece), piece), :]

    ltf[pl.ds(pl.multiple_of(mine + d * piece, piece), piece), :] = total.astype(ltf.dtype)
    for k in range(1, n_d):
        there = lax.rem(d + k, n_d)
        remote(slot(core, d), slot(core, d), g_send, g_recv.at[k - 1], {"dp": there}).start()
    for layer in range(1, layers):
        moment_of_chip(layer)
    for k in range(layers - 1):
        need_group(k)
        add_far(k, 0, own, False)
    with jax.named_scope("gather_wait"):
        for k in range(n_d):
            source = lax.rem(d + n_d - k, n_d)
            if k > 0:
                remote(
                    slot(core, source), slot(core, source), g_send, g_recv.at[k - 1], {"dp": source}
                ).wait_recv()
            remote(slot(core, source), slot(core, source), h_sems.at[0], h_sems.at[1], {"tensor": partner}).start()
        here = ltf.at[pl.ds(other, half), :]
        remote(here, here, h_sems.at[0], h_sems.at[1], {"tensor": partner}).wait()

    slots_out = ltf.at[pl.ds(0, (n_d - 1) * piece), :]
    lanes = lax.broadcasted_iota(jnp.int32, (1, wide), 1) // rank
    sublanes = lax.broadcasted_iota(jnp.int32, (wide, 1), 0) // rank

    def merge(parts, index):
        value = parts[0]
        for layer in range(1, layers):
            value = jnp.where(index == layer, parts[layer], value)
        return value

    with jax.named_scope("token_right"):
        terms = dot(y_chip[layers - 1, my_rows, :], ltf[...], ((1,), (0,)))
        packed = []
        for k in range(layers):
            part = terms[k * pack : (k + 1) * pack]
            packed.append(part if k == layers - 1 else pltpu.roll(part, (k + 1) * rank, 1))
        q_own[...] = merge(packed, lanes).astype(q_own.dtype)
    q_out = []
    for m in range(1, n_y):
        copy = remote(
            q_own, q_far.at[m - 1, core], q_send.at[m - 1], q_recv.at[m - 1], {"tensor": lax.rem(t + 2 * m, n_t)}
        )
        copy.start()
        q_out.append(copy)
    send_chunks(total_chunks)
    with jax.named_scope("right_of_chip"):
        right = merge([dot(ltf[...], m_ref[layer], ((0,), (0,))) for layer in range(layers)], sublanes)
    pass_chunks(sum(PLAN))
    with jax.named_scope("token_right_wait"):
        q_pass = []
        for m in range(1, n_y):
            here = q_far.at[m - 1, core]
            remote(q_own, here, q_send.at[m - 1], q_recv.at[m - 1], {"tensor": lax.rem(t + 2 * m, n_t)}).wait_recv()
            copy = remote(here, here, qf_send.at[m - 1], qf_recv.at[m - 1], {"tensor": partner})
            copy.start()
            q_pass.append(copy)
        for m in range(1, n_y):
            here = q_far.at[m - 1, 1 - core]
            remote(here, here, qf_send.at[m - 1], qf_recv.at[m - 1], {"tensor": partner}).wait_recv()
    far_right = jnp.zeros((rank, feats), F32)
    for m in range(1, n_y):
        basis = q_far[m - 1].reshape(2 * pack, wide)
        for k in range(layers):
            rows = [
                x_ref[layers - 1, pl.ds(pl.multiple_of(far_place(m) * pair + side * own + k * pack, 16), pack), :]
                for side in range(2)
            ]
            term = dot(basis, jnp.concatenate(rows, axis=0), ((0,), (0,)))
            far_right = far_right + term[k * rank : (k + 1) * rank]
    right = jnp.concatenate([right[: wide - rank], right[wide - rank :] + far_right], axis=0)
    share = wide // n_d
    for j in range(n_d):
        r_send[j] = right[j * share : (j + 1) * share, :].astype(BF16)
    for k in range(1, n_d):
        there = lax.rem(d + k, n_d)
        remote(r_send.at[there], r_in.at[k - 1], a_sems.at[0], a_sems.at[1], {"dp": there}).start()

    with jax.named_scope("inverse"):
        gram = dot(ltf[...], ltf[...], ((0,), (0,)))
        grams = [gram[k * rank : (k + 1) * rank, k * rank : (k + 1) * rank] for k in range(layers)]
        inverses = [
            lax.dot_general(
                factor, factor, (((0,), (0,)), ((), ())), precision=HIGHEST, preferred_element_type=F32
            )
            for factor in inverse_factors(grams)
        ]
    with jax.named_scope("right_wait"):
        remote(r_in, r_in, a_sems.at[0], a_sems.at[1], next_d).wait()
    total = r_send[d].astype(F32)
    for k in range(n_d - 1):
        total = total + r_in[k].astype(F32)
    r_all[n_d - 1] = total.astype(BF16)
    for k in range(1, n_d):
        there = lax.rem(d + k, n_d)
        remote(r_all.at[n_d - 1], r_all.at[k - 1], b_sems.at[0], b_sems.at[1], {"dp": there}).start()
    need_group(len(groups) - 3)
    add_far(layers - 1, 0, middle, False)
    with jax.named_scope("right_gather_wait"):
        gathered = r_all.at[pl.ds(0, n_d - 1)]
        remote(gathered, gathered, b_sems.at[0], b_sems.at[1], next_d).wait()
    for source in range(n_d):
        s_all[source * share : (source + 1) * share, :] = r_all[lax.rem(d + n_d - 1 - source, n_d)].astype(F32)
    t_err[...] = jnp.zeros_like(t_err)
    for layer in range(layers):
        rows = pl.ds(layer * rank, rank)
        scaled = lax.dot_general(
            inverses[layer],
            s_all[layer * rank : (layer + 1) * rank, :],
            (((1,), (0,)), ((), ())),
            precision=HIGHEST,
            preferred_element_type=F32,
        )
        high, low = split(scaled * (-1.0 / n_d))
        t_err[layer, layer * rank : (layer + 1) * rank, :] = high
        t_err[layer, wide + layer * rank : wide + (layer + 1) * rank, :] = low

    for layer in range(layers):
        pass_chunks(total_chunks - PASS_LATE + layer)
        add_far(layer, 0, 0, True)
    own_rows = width // n_d
    for layer in range(layers):
        value = low_rank(pl.ds(pl.multiple_of(d * own_rows, own_rows), own_rows), layer)
        sum_ref[layer] = (value * (-1.0 * n_d)).astype(sum_ref.dtype)
    for m in range(1, n_y):
        for side in range(2):
            rows = pl.ds(pl.multiple_of(far_place(m) * pair + side * own + main, 16), tail)
            xt_ref[m - 1, side] = x_ref[layers - 1, rows, :]
    with jax.named_scope("far_wait"):
        need_group(len(groups) - 2)
    add_far(layers - 1, middle, main, False)
    own_copy.wait_send()
    remote(slots_out, slots_out, g_send, h_sems.at[1], next_d).wait_send()
    for copy in q_out + q_pass:
        copy.wait_send()
    with jax.named_scope("tail_wait"):
        need_group(len(groups) - 1)
    whole = y_chip.at[:, my_rows, :]
    for m in range(1, n_y):
        remote(whole, whole, y_send.at[m - 1], y_recv.at[m - 1, 0], next_d).wait_send()
        remote(whole, whole, f_send.at[m - 1], f_recv.at[m - 1, 0], next_d).wait_send()


def finish_kernel(m_ref, sum_ref, yt_ref, xt_ref, err_hbm, out_hbm, stage, m_sems, sum_sem, block_sems):
    layers, width, feats = m_ref.shape
    block_rows = width // BLOCKS
    copies = [pltpu.make_async_copy(m_ref.at[layer], err_hbm.at[layer], m_sems.at[layer]) for layer in range(layers - 1)]
    copies.append(pltpu.make_async_copy(sum_ref, out_hbm, sum_sem))
    for copy in copies:
        copy.start()
    rows = xt_ref.shape[0] * xt_ref.shape[1] * xt_ref.shape[2]
    x_rows = xt_ref[...].reshape(rows, feats)
    for i in range(BLOCKS):
        at = pl.ds(i * block_rows, block_rows)
        term = dot(yt_ref[:, :, :, at].reshape(rows, block_rows), x_rows, ((0,), (0,)))
        stage[at, :] = (m_ref[layers - 1, at, :].astype(F32) + term).astype(stage.dtype)
        copy = pltpu.make_async_copy(stage.at[at, :], err_hbm.at[layers - 1, at, :], block_sems.at[i])
        copy.start()
        copies.append(copy)
    for copy in copies:
        copy.wait()


def solution(mesh):
    n_d, n_t = mesh.shape["dp"], mesh.shape["tensor"]

    def body(context, out_grad, error_in, right_init):
        layers, tokens, feats = context.shape
        own, width = out_grad.shape[1:]
        rank = right_init.shape[1]
        wide = layers * rank
        half = width // 2
        piece = half // n_d
        share = wide // n_d
        n_y = n_t // 2
        far = max(n_y - 1, 1)
        n_c = layers * (own // LAST_ROWS)
        rows = width // n_d
        dma = pltpu.SemaphoreType.DMA
        any_spec = pl.BlockSpec(memory_space=pl.ANY)
        vmem_spec = pl.BlockSpec(memory_space=pltpu.VMEM)
        pairs = lambda *shape: [dma(shape), dma(shape)]
        moment, summed, y_tail, x_tail = pl.pallas_call(
            functools.partial(comm_kernel, n_d, n_t),
            name="low_rank_chain",
            out_shape=(
                pltpu.VMEM((layers, width, feats), BF16),
                pltpu.VMEM((layers, rows, feats), BF16),
                pltpu.VMEM((far, 2, TAIL, width), BF16),
                pltpu.VMEM((far, 2, TAIL, feats), BF16),
            ),
            in_specs=[any_spec] * 4,
            out_specs=(vmem_spec,) * 4,
            scratch_shapes=[
                pltpu.VMEM((layers, tokens, feats), BF16),
                pltpu.VMEM((layers, 2 * own, width), BF16),
                pltpu.VMEM((layers, far, 2, own, width), BF16),
                pltpu.VMEM((layers, rank, feats), F32),
                pltpu.VMEM((2, n_y, own, wide), F32),
                pltpu.VMEM((n_y, own, wide), F32),
                pltpu.VMEM((far, own, wide), WIRE),
                pltpu.VMEM((far, own, wide), WIRE),
                pltpu.VMEM((own // layers, wide), WIRE),
                pltpu.VMEM((far, 2, own // layers, wide), WIRE),
                pltpu.VMEM((width, wide), F32),
                pltpu.VMEM((half, wide), F32),
                pltpu.VMEM((n_d, piece, wide), WIRE),
                pltpu.VMEM((n_d - 1, piece, wide), WIRE),
                pltpu.VMEM((n_y, piece, wide), WIRE),
                pltpu.VMEM((width, wide), WIRE),
                pltpu.VMEM((n_d, share, feats), BF16),
                pltpu.VMEM((n_d - 1, share, feats), BF16),
                pltpu.VMEM((n_d, share, feats), BF16),
                pltpu.VMEM((wide, feats), F32),
                pltpu.VMEM((layers, 2 * wide, feats), BF16),
                dma((3,)),
                dma((2, layers)),
            ]
            + [dma((far,)), dma((far, n_c)), dma((far,)), dma((far, layers + 2)), dma((2,))]
            + pairs(far)
            + [dma((2,)), dma((2,)), dma((2,))]
            + pairs(far)
            + [dma, dma((n_d - 1,)), dma((2,))]
            + pairs(far)
            + pairs(far)
            + [dma((2,)), dma((2,))]
            + [pltpu.SemaphoreType.REGULAR, pltpu.SemaphoreType.REGULAR],
            compiler_params=pltpu.CompilerParams(
                collective_id=0, has_side_effects=True, vmem_limit_bytes=40 * 1024 * 1024
            ),
        )(*(pltpu.with_memory_space_constraint(a, pltpu.HBM) for a in (context, out_grad, error_in, right_init)))
        new_error, total = pl.pallas_call(
            finish_kernel,
            name="new_error",
            in_specs=[vmem_spec] * 4,
            out_specs=(any_spec, any_spec),
            out_shape=(
                jax.ShapeDtypeStruct((layers, width, feats), BF16),
                jax.ShapeDtypeStruct((layers, rows, feats), BF16),
            ),
            scratch_shapes=[pltpu.VMEM((width, feats), BF16), dma((layers,)), dma, dma((BLOCKS,))],
            compiler_params=pltpu.CompilerParams(vmem_limit_bytes=16 * 1024 * 1024),
        )(moment, summed, y_tail, x_tail)
        return total, new_error

    return jax.shard_map(
        body,
        mesh=mesh,
        in_specs=(
            P(None, "dp", "tensor"),
            P(None, ("dp", "tensor"), None),
            P(None, "dp", "tensor"),
            P(None, None, "tensor"),
        ),
        out_specs=(P(None, "dp", "tensor"), P(None, "dp", "tensor")),
        check_vma=False,
    )
```

```python
import functools

import jax
import jax.numpy as jnp
from jax import lax
from jax.experimental import pallas as pl
from jax.experimental.pallas import tpu as pltpu
from jax.sharding import PartitionSpec as P

MESH = pl.DeviceIdType.MESH
HIGHEST = lax.Precision.HIGHEST
F32 = jnp.float32
BF16 = jnp.bfloat16
WIRE = jnp.bfloat16
ROWS = 16
LAST_ROWS = 16
PASSED = 9
PASS_LATE = 4
BLOCKS = 6
PLAN = (2, 7, 4, 8)


def split(value):
    high = value.astype(BF16)
    return high, (value - high.astype(F32)).astype(BF16)


def dot(a, b, dims):
    return lax.dot_general(a, b, (dims, ((), ())), preferred_element_type=F32)


def inverse_factors(grams):
    size = grams[0].shape[0]
    rows = lax.broadcasted_iota(jnp.int32, (size, size), 0)
    cols = lax.broadcasted_iota(jnp.int32, (size, size), 1)
    eye = (rows == cols).astype(F32)
    wide_rows = lax.broadcasted_iota(jnp.int32, (size, 2 * size), 0)
    work = []
    for gram in grams:
        mean = jnp.sum(jnp.sum(gram * eye, axis=1, keepdims=True), axis=0, keepdims=True) / size
        work.append(jnp.concatenate([gram + (1e-06 * mean) * eye, eye], axis=1))
    scales = [jnp.zeros((size, 1), F32) for _ in grams]
    one_col = wide_rows[:, :1]
    for k in range(size):
        for i, full in enumerate(work):
            row = full[k : k + 1, :]
            pivot = full[k : k + 1, k : k + 1]
            ratio = jnp.where(one_col > k, full[:, k : k + 1] / pivot, 0.0)
            scales[i] = jnp.where(one_col == k, lax.rsqrt(pivot), scales[i])
            work[i] = full - ratio * row
    return [full[:, size:] * scale for full, scale in zip(work, scales)]


def fold(parts, rank):
    if len(parts) == 2:
        first = lax.broadcasted_iota(jnp.int32, (1, 2 * rank), 1) < rank
        kept = jnp.where(first, parts[0], parts[1])
        moved = jnp.where(first, parts[1], parts[0])
        return kept + pltpu.roll(moved, rank, 1)
    return jnp.concatenate([part[:, :rank] + part[:, rank:] for part in parts], axis=1)


def comm_kernel(
    n_d,
    n_t,
    x_hbm,
    y_hbm,
    e_hbm,
    r_hbm,
    m_ref,
    sum_ref,
    yt_ref,
    xt_ref,
    x_ref,
    y_chip,
    y_far,
    r_ref,
    pt,
    pt_core,
    pt_send,
    pt_in,
    q_own,
    q_far,
    lt,
    lt_core,
    lt_send,
    lt_in,
    lt_y,
    ltf,
    r_send,
    r_in,
    r_all,
    s_all,
    t_err,
    local_sems,
    e_sems,
    y_send,
    y_recv,
    f_send,
    f_recv,
    own_sems,
    p_send,
    p_recv,
    pc_sems,
    c_sems,
    d_sems,
    s_send,
    s_recv,
    g_send,
    g_recv,
    h_sems,
    q_send,
    q_recv,
    qf_send,
    qf_recv,
    a_sems,
    b_sems,
    go_tensor,
    go_dp,
):
    layers, own, width = y_hbm.shape
    tokens, feats = x_ref.shape[1:]
    rank = r_ref.shape[1]
    wide = layers * rank
    d = lax.axis_index("dp")
    t = lax.axis_index("tensor")
    core = lax.rem(t, 2)
    place = lax.div(t, 2)
    partner = t + 1 - 2 * core
    n_y = n_t // 2
    half = width // 2
    piece = half // n_d
    block_rows = width // BLOCKS
    pair = 2 * own
    pack = own // layers
    tail = own // 4
    main = own - tail

    def remote(src, dst, send, recv, where):
        return pltpu.make_async_remote_copy(
            src_ref=src, dst_ref=dst, send_sem=send, recv_sem=recv, device_id=where, device_id_type=MESH
        )

    my_rows = pl.ds(pl.multiple_of(core * own, own), own)
    partner_rows = pl.ds(pl.multiple_of((1 - core) * own, own), own)

    barrier = pltpu.get_barrier_semaphore()
    for k in range(1, n_t):
        there = lax.rem(t + k, n_t)

        @pl.when(lax.rem(there, 2) == 0)
        def _():
            pl.semaphore_signal(barrier, inc=1, device_id={"tensor": there}, device_id_type=MESH)

    r_load = pltpu.make_async_copy(r_hbm, r_ref, local_sems.at[0])
    x_load = pltpu.make_async_copy(x_hbm, x_ref, local_sems.at[1])
    y_load = pltpu.make_async_copy(y_hbm, y_chip.at[:, my_rows, :], local_sems.at[2])
    e_loads = []
    for side in range(2):
        at = pl.ds(side * half, half)
        for layer in range(layers):
            e_loads.append(
                pltpu.make_async_copy(e_hbm.at[layer, at, :], m_ref.at[layer, at, :], e_sems.at[side, layer])
            )
    with jax.named_scope("bar"):

        @pl.when(core == 0)
        def _():
            pl.semaphore_wait(barrier, n_t - 1)
            pl.semaphore_signal(go_tensor, inc=1, device_id={"tensor": partner}, device_id_type=MESH)

        @pl.when(core == 1)
        def _():
            pl.semaphore_wait(go_tensor, 1)
            for k in range(1, n_d):
                pl.semaphore_signal(barrier, inc=1, device_id={"dp": lax.rem(d + k, n_d)}, device_id_type=MESH)

    chunks = []
    for layer in range(layers):
        row = 0
        while row < own:
            count = ROWS if layer < layers - 1 or row < main else LAST_ROWS
            chunks.append((layer, row, count))
            row += count
    total_chunks = len(chunks)

    def landing(i, m, side):
        layer, row, count = chunks[i]
        if layer == layers - 1 and row >= main:
            return yt_ref.at[m - 1, side, pl.ds(row - main, count), :]
        return y_far.at[layer, m - 1, side, pl.ds(row, count), :]

    def chunk_copy(i, m):
        layer, row, count = chunks[i]
        return remote(
            y_hbm.at[layer, pl.ds(row, count), :],
            landing(i, m, core),
            y_send.at[m - 1],
            y_recv.at[m - 1, i],
            {"tensor": lax.rem(t + 2 * m, n_t)},
        )

    middle = own // 2
    groups = [(layer, 0, own) for layer in range(layers - 1)]
    groups += [(layers - 1, 0, middle), (layers - 1, middle, main), (layers - 1, main, own)]

    def group_of(i):
        layer, row, _ = chunks[i]
        return [k for k, g in enumerate(groups) if g[0] == layer and g[1] <= row < g[2]][0]

    def forward_copy(i, m):
        here = landing(i, m, core)
        return remote(here, here, f_send.at[m - 1], f_recv.at[m - 1, group_of(i)], {"tensor": partner})

    def group_in(k, m):
        layer, start, stop = groups[k]
        if k == len(groups) - 1:
            here = yt_ref.at[m - 1, 1 - core]
        else:
            here = y_far.at[layer, m - 1, 1 - core, pl.ds(start, stop - start), :]
        return remote(here, here, f_send.at[m - 1], f_recv.at[m - 1, k], {"tensor": partner})

    sent = [0]
    passed = [0]

    def send_chunks(count):
        stop = min(sent[0] + count, total_chunks)
        for i in range(sent[0], stop):
            for m in range(1, n_y):
                chunk_copy(i, m).start()
        sent[0] = stop

    def pass_chunks(upto):
        for i in range(passed[0], min(upto, sent[0])):
            for m in range(1, n_y):
                chunk_copy(i, m).wait_recv()
                forward_copy(i, m).start()
        passed[0] = max(passed[0], min(upto, sent[0]))

    def need_group(k):
        for i in range(total_chunks):
            if group_of(i) <= k:
                pass_chunks(i + 1)
        for m in range(1, n_y):
            group_in(k, m).wait_recv()

    send_chunks(PLAN[0])
    own_copy = remote(y_hbm, y_chip.at[:, my_rows, :], own_sems.at[0], own_sems.at[1], {"tensor": partner})
    own_in = remote(y_hbm, y_chip.at[:, partner_rows, :], own_sems.at[0], own_sems.at[1], {"tensor": partner})

    r_load.start()
    x_load.start()
    def far_place(m):
        return lax.rem(place + n_y - m, n_y)

    r_load.wait()
    x_load.wait()
    for load in e_loads:
        load.start()
    y_load.start()
    r_parts = []
    for layer in range(layers):
        high, low = split(r_ref[layer])
        r_parts.append(jnp.concatenate([high, low] if layer % 2 == 0 else [low, high], axis=0))
    with jax.named_scope("token_terms"):
        for side in range(2):
            for other in range(n_y):
                at = pl.ds((2 * other + side) * own, own)
                parts = [dot(x_ref[layer, at, :], r_parts[layer], ((1,), (1,))) for layer in range(layers)]
                pt[side, other] = fold(parts, rank)
    pc_copy = remote(pt.at[1 - core], pt_core, pc_sems.at[0], pc_sems.at[1], {"tensor": partner})
    pc_copy.start()
    pc_copy.wait()
    p_total = None
    for m in range(1, n_y):
        there = lax.rem(place + m, n_y)
        pt_send[m - 1] = (pt[core, there] + pt_core[there]).astype(WIRE)
    p_out = []
    for m in range(1, n_y):
        copy = remote(
            pt_send.at[m - 1], pt_in.at[m - 1], p_send.at[m - 1], p_recv.at[m - 1], {"tensor": lax.rem(t + 2 * m, n_t)}
        )
        copy.start()
        p_out.append(copy)
    send_chunks(PLAN[1])
    p_total = pt[core, place] + pt_core[place]

    with jax.named_scope("left_of_error"):
        for side in range(2):
            for load in e_loads[side * layers : (side + 1) * layers]:
                load.wait()

            def left_of_error(i, carry):
                at = pl.ds(pl.multiple_of(side * half + i * block_rows, block_rows), block_rows)
                parts = [dot(m_ref[layer, at, :], r_parts[layer], ((1,), (1,))) for layer in range(layers)]
                lt[at, :] = fold(parts, rank)
                return carry

            lax.fori_loop(0, BLOCKS // 2, left_of_error, 0)
    y_load.wait()
    own_copy.start()
    with jax.named_scope("token_wait"):
        for copy in p_out:
            copy.wait()
    for m in range(1, n_y):
        p_total = p_total + pt_in[m - 1].astype(F32)
    p_high = p_total.astype(BF16).astype(F32)
    p_low = p_total - p_high
    if layers == 2:
        first = lax.broadcasted_iota(jnp.int32, (1, wide), 1) < rank
        turned = pltpu.roll(p_low, rank, 1)
        p_parts = [jnp.where(first, p_high, turned).astype(BF16), jnp.where(first, turned, p_high).astype(BF16)]
    else:
        p_parts = [
            jnp.concatenate([part[:, k * rank : (k + 1) * rank] for part in (p_high, p_low)], axis=1).astype(BF16)
            for k in range(layers)
        ]

    mine = pl.multiple_of(core * half, half)
    other = pl.multiple_of((1 - core) * half, half)

    def left_of_tokens(start):
        def step(i, carry):
            at = pl.ds(pl.multiple_of(start + i * block_rows, block_rows), block_rows)
            parts = [dot(y_chip[layer, my_rows, at], p_parts[layer], ((0,), (0,))) for layer in range(layers)]
            lt[at, :] += fold(parts, rank)
            return carry

        lax.fori_loop(0, BLOCKS // 2, step, 0)

    core_copy = remote(lt.at[pl.ds(other, half), :], lt_core, c_sems.at[0], c_sems.at[1], {"tensor": partner})
    with jax.named_scope("left_of_tokens"):
        left_of_tokens(other)
        core_copy.start()
        left_of_tokens(mine)
    with jax.named_scope("core_wait"):
        core_copy.wait()

    def add_core(j, carry):
        at = pl.ds(pl.multiple_of(mine + j * piece, piece), piece)
        value = lt[at, :] + lt_core[pl.ds(pl.multiple_of(j * piece, piece), piece), :]
        lt_send[j] = value.astype(lt_send.dtype)
        return carry

    lax.fori_loop(0, n_d, add_core, 0)
    with jax.named_scope("bar_dp"):

        @pl.when(core == 1)
        def _():
            pl.semaphore_wait(barrier, n_d - 1)
            pl.semaphore_signal(go_dp, inc=1, device_id={"tensor": partner}, device_id_type=MESH)

        @pl.when(core == 0)
        def _():
            pl.semaphore_wait(go_dp, 1)

    next_d = {"dp": lax.rem(d + 1, n_d)}
    for k in range(1, n_d):
        there = lax.rem(d + k, n_d)
        remote(lt_send.at[there], lt_in.at[k - 1], d_sems.at[0], d_sems.at[1], {"dp": there}).start()
    send_chunks(PLAN[2])

    def moment_of_chip(layer):
        tokens_here = pl.ds(pl.multiple_of(place * pair, pair), pair)

        def step(i, carry):
            at = pl.ds(pl.multiple_of(i * block_rows, block_rows), block_rows)
            term = dot(y_chip[layer, :, at], x_ref[layer, tokens_here, :], ((0,), (0,)))
            m_ref[layer, at, :] = (m_ref[layer, at, :].astype(F32) + term).astype(BF16)
            return carry

        with jax.named_scope("moment"):
            lax.fori_loop(0, BLOCKS, step, 0)

    def low_rank(at, layer):
        basis = ltf[at, :]
        return dot(jnp.concatenate([basis, basis], axis=1), t_err[layer], ((1,), (0,)))

    def add_far(layer, start, stop, with_rank):
        def step(i, carry):
            at = pl.ds(pl.multiple_of(i * block_rows, block_rows), block_rows)
            value = m_ref[layer, at, :].astype(F32)
            if with_rank:
                value = value + low_rank(at, layer)
            for m in range(1, n_y):
                base = far_place(m) * pair
                if stop == start:
                    continue
                y_rows = [y_far[layer, m - 1, side, start:stop, at] for side in range(2)]
                x_rows = [
                    x_ref[layer, pl.ds(pl.multiple_of(base + side * own + start, 16), stop - start), :]
                    for side in range(2)
                ]
                value = value + dot(jnp.concatenate(y_rows, axis=0), jnp.concatenate(x_rows, axis=0), ((0,), (0,)))
            m_ref[layer, at, :] = value.astype(BF16)
            return carry

        with jax.named_scope("far_terms"):
            lax.fori_loop(0, BLOCKS, step, 0)

    own_in.wait_recv()
    moment_of_chip(0)
    with jax.named_scope("dp_wait"):
        remote(lt_in, lt_in, d_sems.at[0], d_sems.at[1], next_d).wait()
    total = lt[pl.ds(pl.multiple_of(mine + d * piece, piece), piece), :]
    total = total + lt_core[pl.ds(pl.multiple_of(d * piece, piece), piece), :]
    for k in range(n_d - 1):
        total = total + lt_in[k].astype(F32)
    lt_y[n_y - 1] = total.astype(lt_y.dtype)
    s_out = []
    for m in range(1, n_y):
        copy = remote(lt_y.at[n_y - 1], lt_y.at[m - 1], s_send.at[m - 1], s_recv.at[m - 1], {"tensor": lax.rem(t + 2 * m, n_t)})
        copy.start()
        s_out.append(copy)
    send_chunks(PLAN[3])
    pass_chunks(PASSED)
    with jax.named_scope("sum_wait"):
        for copy in s_out:
            copy.wait()
    total = lt_y[lax.rem(place + n_y - 1, n_y)].astype(F32)
    for source in range(1, n_y):
        total = total + lt_y[lax.rem(place + 2 * n_y - 1 - source, n_y)].astype(F32)

    def slot(side, index):
        return ltf.at[pl.ds(pl.multiple_of(side * half + index * piece, piece), piece), :]

    ltf[pl.ds(pl.multiple_of(mine + d * piece, piece), piece), :] = total.astype(ltf.dtype)
    for k in range(1, n_d):
        there = lax.rem(d + k, n_d)
        remote(slot(core, d), slot(core, d), g_send, g_recv.at[k - 1], {"dp": there}).start()
    for layer in range(1, layers):
        moment_of_chip(layer)
    for k in range(layers - 1):
        need_group(k)
        add_far(k, 0, own, False)
    with jax.named_scope("gather_wait"):
        for k in range(n_d):
            source = lax.rem(d + n_d - k, n_d)
            if k > 0:
                remote(
                    slot(core, source), slot(core, source), g_send, g_recv.at[k - 1], {"dp": source}
                ).wait_recv()
            remote(slot(core, source), slot(core, source), h_sems.at[0], h_sems.at[1], {"tensor": partner}).start()
        here = ltf.at[pl.ds(other, half), :]
        remote(here, here, h_sems.at[0], h_sems.at[1], {"tensor": partner}).wait()

    slots_out = ltf.at[pl.ds(0, (n_d - 1) * piece), :]
    lanes = lax.broadcasted_iota(jnp.int32, (1, wide), 1) // rank
    sublanes = lax.broadcasted_iota(jnp.int32, (wide, 1), 0) // rank

    def merge(parts, index):
        value = parts[0]
        for layer in range(1, layers):
            value = jnp.where(index == layer, parts[layer], value)
        return value

    with jax.named_scope("token_right"):
        terms = dot(y_chip[layers - 1, my_rows, :], ltf[...], ((1,), (0,)))
        packed = []
        for k in range(layers):
            part = terms[k * pack : (k + 1) * pack]
            packed.append(part if k == layers - 1 else pltpu.roll(part, (k + 1) * rank, 1))
        q_own[...] = merge(packed, lanes).astype(q_own.dtype)
    q_out = []
    for m in range(1, n_y):
        copy = remote(
            q_own, q_far.at[m - 1, core], q_send.at[m - 1], q_recv.at[m - 1], {"tensor": lax.rem(t + 2 * m, n_t)}
        )
        copy.start()
        q_out.append(copy)
    send_chunks(total_chunks)
    with jax.named_scope("right_of_chip"):
        right = merge([dot(ltf[...], m_ref[layer], ((0,), (0,))) for layer in range(layers)], sublanes)
    pass_chunks(sum(PLAN))
    with jax.named_scope("token_right_wait"):
        q_pass = []
        for m in range(1, n_y):
            here = q_far.at[m - 1, core]
            remote(q_own, here, q_send.at[m - 1], q_recv.at[m - 1], {"tensor": lax.rem(t + 2 * m, n_t)}).wait_recv()
            copy = remote(here, here, qf_send.at[m - 1], qf_recv.at[m - 1], {"tensor": partner})
            copy.start()
            q_pass.append(copy)
        for m in range(1, n_y):
            here = q_far.at[m - 1, 1 - core]
            remote(here, here, qf_send.at[m - 1], qf_recv.at[m - 1], {"tensor": partner}).wait_recv()
    far_right = jnp.zeros((rank, feats), F32)
    for m in range(1, n_y):
        basis = q_far[m - 1].reshape(2 * pack, wide)
        for k in range(layers):
            rows = [
                x_ref[layers - 1, pl.ds(pl.multiple_of(far_place(m) * pair + side * own + k * pack, 16), pack), :]
                for side in range(2)
            ]
            term = dot(basis, jnp.concatenate(rows, axis=0), ((0,), (0,)))
            far_right = far_right + term[k * rank : (k + 1) * rank]
    right = jnp.concatenate([right[: wide - rank], right[wide - rank :] + far_right], axis=0)
    share = wide // n_d
    for j in range(n_d):
        r_send[j] = right[j * share : (j + 1) * share, :].astype(BF16)
    for k in range(1, n_d):
        there = lax.rem(d + k, n_d)
        remote(r_send.at[there], r_in.at[k - 1], a_sems.at[0], a_sems.at[1], {"dp": there}).start()

    with jax.named_scope("inverse"):
        gram = dot(ltf[...], ltf[...], ((0,), (0,)))
        grams = [gram[k * rank : (k + 1) * rank, k * rank : (k + 1) * rank] for k in range(layers)]
        inverses = [
            lax.dot_general(
                factor, factor, (((0,), (0,)), ((), ())), precision=HIGHEST, preferred_element_type=F32
            )
            for factor in inverse_factors(grams)
        ]
    with jax.named_scope("right_wait"):
        remote(r_in, r_in, a_sems.at[0], a_sems.at[1], next_d).wait()
    total = r_send[d].astype(F32)
    for k in range(n_d - 1):
        total = total + r_in[k].astype(F32)
    r_all[n_d - 1] = total.astype(BF16)
    for k in range(1, n_d):
        there = lax.rem(d + k, n_d)
        remote(r_all.at[n_d - 1], r_all.at[k - 1], b_sems.at[0], b_sems.at[1], {"dp": there}).start()
    need_group(len(groups) - 3)
    add_far(layers - 1, 0, middle, False)
    with jax.named_scope("right_gather_wait"):
        gathered = r_all.at[pl.ds(0, n_d - 1)]
        remote(gathered, gathered, b_sems.at[0], b_sems.at[1], next_d).wait()
    for source in range(n_d):
        s_all[source * share : (source + 1) * share, :] = r_all[lax.rem(d + n_d - 1 - source, n_d)].astype(F32)
    t_err[...] = jnp.zeros_like(t_err)
    for layer in range(layers):
        rows = pl.ds(layer * rank, rank)
        scaled = lax.dot_general(
            inverses[layer],
            s_all[layer * rank : (layer + 1) * rank, :],
            (((1,), (0,)), ((), ())),
            precision=HIGHEST,
            preferred_element_type=F32,
        )
        high, low = split(scaled * (-1.0 / n_d))
        t_err[layer, layer * rank : (layer + 1) * rank, :] = high
        t_err[layer, wide + layer * rank : wide + (layer + 1) * rank, :] = low

    for layer in range(layers):
        pass_chunks(total_chunks - PASS_LATE + layer)
        add_far(layer, 0, 0, True)
    own_rows = width // n_d
    for layer in range(layers):
        value = low_rank(pl.ds(pl.multiple_of(d * own_rows, own_rows), own_rows), layer)
        sum_ref[layer] = (value * (-1.0 * n_d)).astype(sum_ref.dtype)
    for m in range(1, n_y):
        for side in range(2):
            rows = pl.ds(pl.multiple_of(far_place(m) * pair + side * own + main, 16), tail)
            xt_ref[m - 1, side] = x_ref[layers - 1, rows, :]
    with jax.named_scope("far_wait"):
        need_group(len(groups) - 2)
    add_far(layers - 1, middle, main, False)
    own_copy.wait_send()
    remote(slots_out, slots_out, g_send, h_sems.at[1], next_d).wait_send()
    for copy in q_out + q_pass:
        copy.wait_send()
    with jax.named_scope("tail_wait"):
        need_group(len(groups) - 1)
    whole = y_chip.at[:, my_rows, :]
    for m in range(1, n_y):
        remote(whole, whole, y_send.at[m - 1], y_recv.at[m - 1, 0], next_d).wait_send()
        remote(whole, whole, f_send.at[m - 1], f_recv.at[m - 1, 0], next_d).wait_send()


def finish_kernel(m_ref, sum_ref, yt_ref, xt_ref, err_hbm, out_hbm, stage, m_sems, sum_sem, block_sems):
    layers, width, feats = m_ref.shape
    block_rows = width // BLOCKS
    copies = [pltpu.make_async_copy(m_ref.at[layer], err_hbm.at[layer], m_sems.at[layer]) for layer in range(layers - 1)]
    copies.append(pltpu.make_async_copy(sum_ref, out_hbm, sum_sem))
    for copy in copies:
        copy.start()
    rows = xt_ref.shape[0] * xt_ref.shape[1] * xt_ref.shape[2]
    x_rows = xt_ref[...].reshape(rows, feats)
    for i in range(BLOCKS):
        at = pl.ds(i * block_rows, block_rows)
        term = dot(yt_ref[:, :, :, at].reshape(rows, block_rows), x_rows, ((0,), (0,)))
        stage[at, :] = (m_ref[layers - 1, at, :].astype(F32) + term).astype(stage.dtype)
        copy = pltpu.make_async_copy(stage.at[at, :], err_hbm.at[layers - 1, at, :], block_sems.at[i])
        copy.start()
        copies.append(copy)
    for copy in copies:
        copy.wait()


def solution(mesh):
    n_d, n_t = mesh.shape["dp"], mesh.shape["tensor"]

    def body(context, out_grad, error_in, right_init):
        layers, tokens, feats = context.shape
        own, width = out_grad.shape[1:]
        rank = right_init.shape[1]
        wide = layers * rank
        half = width // 2
        piece = half // n_d
        share = wide // n_d
        n_y = n_t // 2
        far = max(n_y - 1, 1)
        n_c = layers * (own // LAST_ROWS)
        rows = width // n_d
        dma = pltpu.SemaphoreType.DMA
        any_spec = pl.BlockSpec(memory_space=pl.ANY)
        vmem_spec = pl.BlockSpec(memory_space=pltpu.VMEM)
        pairs = lambda *shape: [dma(shape), dma(shape)]
        moment, summed, y_tail, x_tail = pl.pallas_call(
            functools.partial(comm_kernel, n_d, n_t),
            name="low_rank_chain",
            out_shape=(
                pltpu.VMEM((layers, width, feats), BF16),
                pltpu.VMEM((layers, rows, feats), BF16),
                pltpu.VMEM((far, 2, own // 4, width), BF16),
                pltpu.VMEM((far, 2, own // 4, feats), BF16),
            ),
            in_specs=[any_spec] * 4,
            out_specs=(vmem_spec,) * 4,
            scratch_shapes=[
                pltpu.VMEM((layers, tokens, feats), BF16),
                pltpu.VMEM((layers, 2 * own, width), BF16),
                pltpu.VMEM((layers, far, 2, own, width), BF16),
                pltpu.VMEM((layers, rank, feats), F32),
                pltpu.VMEM((2, n_y, own, wide), F32),
                pltpu.VMEM((n_y, own, wide), F32),
                pltpu.VMEM((far, own, wide), WIRE),
                pltpu.VMEM((far, own, wide), WIRE),
                pltpu.VMEM((own // layers, wide), WIRE),
                pltpu.VMEM((far, 2, own // layers, wide), WIRE),
                pltpu.VMEM((width, wide), F32),
                pltpu.VMEM((half, wide), F32),
                pltpu.VMEM((n_d, piece, wide), WIRE),
                pltpu.VMEM((n_d - 1, piece, wide), WIRE),
                pltpu.VMEM((n_y, piece, wide), WIRE),
                pltpu.VMEM((width, wide), WIRE),
                pltpu.VMEM((n_d, share, feats), BF16),
                pltpu.VMEM((n_d - 1, share, feats), BF16),
                pltpu.VMEM((n_d, share, feats), BF16),
                pltpu.VMEM((wide, feats), F32),
                pltpu.VMEM((layers, 2 * wide, feats), BF16),
                dma((3,)),
                dma((2, layers)),
            ]
            + [dma((far,)), dma((far, n_c)), dma((far,)), dma((far, layers + 2)), dma((2,))]
            + pairs(far)
            + [dma((2,)), dma((2,)), dma((2,))]
            + pairs(far)
            + [dma, dma((n_d - 1,)), dma((2,))]
            + pairs(far)
            + pairs(far)
            + [dma((2,)), dma((2,))]
            + [pltpu.SemaphoreType.REGULAR, pltpu.SemaphoreType.REGULAR],
            compiler_params=pltpu.CompilerParams(
                collective_id=0, has_side_effects=True, vmem_limit_bytes=40 * 1024 * 1024
            ),
        )(*(pltpu.with_memory_space_constraint(a, pltpu.HBM) for a in (context, out_grad, error_in, right_init)))
        new_error, total = pl.pallas_call(
            finish_kernel,
            name="new_error",
            in_specs=[vmem_spec] * 4,
            out_specs=(any_spec, any_spec),
            out_shape=(
                jax.ShapeDtypeStruct((layers, width, feats), BF16),
                jax.ShapeDtypeStruct((layers, rows, feats), BF16),
            ),
            scratch_shapes=[pltpu.VMEM((width, feats), BF16), dma((layers,)), dma, dma((BLOCKS,))],
            compiler_params=pltpu.CompilerParams(vmem_limit_bytes=16 * 1024 * 1024),
        )(moment, summed, y_tail, x_tail)
        return total, new_error

    return jax.shard_map(
        body,
        mesh=mesh,
        in_specs=(
            P(None, "dp", "tensor"),
            P(None, ("dp", "tensor"), None),
            P(None, "dp", "tensor"),
            P(None, None, "tensor"),
        ),
        out_specs=(P(None, "dp", "tensor"), P(None, "dp", "tensor")),
        check_vma=False,
    )
```
